32 devices in a mesh: ep: 16 (over z, y, x), etp: 2 (over core).
Axes of the slice: x: 2, y: 2, z: 4, core: 2. Of those that a mesh axis runs over, the one named last changes fastest.
Arguments:
- tokens: bfloat16 [2048, 3584], P('ep'), may hold values from -6 to 6
- expert_ids: int32 [2048, 8], P('ep'), may hold values from 0 to 15, all different within a row; in each aligned block of 128 rows (0 to 127, 128 to 255, ...) at most 72 rows name the same one
- routing_gates: float32 [2048, 8], P('ep'), may hold values from 0.1 to 1
- w_gate: bfloat16 [16, 3584, 1024], P('ep', None, 'etp'), may hold values from -0.09375 to 0.09375
- w_up: bfloat16 [16, 3584, 1024], P('ep', None, 'etp'), may hold values from -0.09375 to 0.09375
- w_down: bfloat16 [16, 1024, 3584], P('ep', 'etp'), may hold values from -0.1875 to 0.1875
Outputs:
- combined: bfloat16 [2048, 3584], P('ep', 'etp')
The draws below stay inside these ranges and needn't reach their ends.
Inputs may be any that keep to these rules, and one draw needn't show every extreme that they name: `expert_ids`: each row names 8 different experts; within the rows of one index of ep no expert is named by more than 72 rows.
All inputs are finite; a program needn't handle non-finite values.
Results may differ from the reference program's by a relative error of at most 0.008.
Values may be sent and summed in bfloat16 or wider, within the bound.
A program may use at most 128 MiB of HBM per device.

```python
import math
import jax
import jax.numpy as jnp
import numpy as np
from jax import lax

D = 3584
FF = 1024
TOP = 8
TOK_DEV = 128
EXPERTS = 16
TOKENS = 2048
CAP = 72
N_EP = 16
N_ETP = 2


def block_levels(stream_key, dims, cuts, smallest, largest):
    def one(dim, parts):
        heights = jax.random.uniform(jax.random.fold_in(jax.random.fold_in(stream_key, 6), dim), (parts,), jnp.float32, smallest / len(cuts), largest / len(cuts))
        return jnp.repeat(jnp.exp(heights), dims[dim] // parts).reshape((-1,) + (1,) * (len(dims) - dim - 1))

    factor_of = one(*cuts[0])
    for cut in cuts[1:]:
        factor_of = factor_of * one(*cut)
    return factor_of


def assign_block(stream_key, own, number, rows, number_of, top, reach, skew):
    sequence = jax.random.permutation(stream_key, number_of)
    packed, usual = load_shares(number_of, rows * top, reach, skew, True), load_shares(number_of, rows * top, reach, skew, False)
    places = jnp.arange(number_of)

    def named(sizes, offset_by):
        used = int((sizes > 0).sum())
        fixed = max(1, used // 4)
        passed = fixed + (places - fixed + offset_by * (used - fixed)) % max(1, number_of - fixed)
        return jnp.zeros((number_of,), jnp.int32).at[sequence[jnp.where(places < fixed, places, passed)]].set(jnp.asarray(sizes, jnp.int32))

    sizes = jnp.where(number % 4 == 0, named(packed, number // 4), named(usual, number - number // 4 - 1))
    mixed = jax.random.permutation(jax.random.fold_in(own, 3), number_of)
    donor, receiver = mixed[0:number_of // 2 * 2:2], mixed[1:number_of // 2 * 2:2]
    margin = jnp.minimum(sizes[donor] - 1, reach - sizes[receiver]) // 2
    margin = jnp.where((donor == sequence[0]) | (receiver == sequence[0]) | (sizes[receiver] == 0), 0, jnp.maximum(margin, 0))
    passed = jax.random.randint(jax.random.fold_in(own, 4), (number_of // 2,), 0, 1 << 20) % (margin + 1)
    sizes = sizes.at[donor].add(-passed).at[receiver].add(passed)
    members = jnp.searchsorted(jnp.cumsum(sizes), jnp.arange(rows * top), side="right").astype(jnp.int32)
    grid = members.reshape(top, rows).T
    grid = grid[jax.random.permutation(jax.random.fold_in(own, 1), rows)]
    offset_by = jax.random.randint(jax.random.fold_in(own, 2), (rows, 1), 0, top)
    return jnp.take_along_axis(grid, (jnp.arange(top)[None, :] + offset_by) % top, axis=1)


def load_shares(count, total, bound, skew, full):
    loads = [(1 << 20) // math.isqrt(standing ** skew) + 1 for standing in range(1, count + 1)]
    largest = bound if full else min(bound, max(-(-total // count), total * loads[0] // sum(loads)))
    least = 1 if total - largest >= count - 1 else 0
    holding, spare = [largest] + [least] * (count - 1), total - largest - least * (count - 1)
    while spare > 0:
        free = [i for i in range(1, count) if holding[i] < largest] or [i for i in range(1, count) if holding[i] < bound]
        pool, budget = sum([loads[i] for i in free]), spare
        for i in free:
            extra = min(bound - holding[i], max(1, budget * loads[i] // pool), spare)
            holding[i] = holding[i] + extra
            spare = spare - extra
    return np.array(holding)


def bell_draw(own_key, shape, scale, bound, shards=(), kind=jnp.bfloat16):
    factor_of = block_levels(own_key, shape, shards, -0.22, 0.18) if shards else 1.0
    array = jax.random.normal(own_key, shape, jnp.float32) * scale * factor_of
    return jnp.minimum(jnp.maximum(array, -bound), bound).astype(kind)


def setup_inputs(seed: int = 0) -> dict:
    arg_keys = jax.random.split(jax.random.key(seed), 7)
    tokens = bell_draw(arg_keys[0], (TOKENS, D), 1.0, 6.0, ((0, 16),))
    expert_ids_keys = jax.random.split(jax.random.fold_in(arg_keys[1], 1), TOKENS // TOK_DEV)
    expert_ids_turns = jax.random.permutation(jax.random.fold_in(arg_keys[1], 3), TOKENS // TOK_DEV)
    expert_ids = jax.vmap(lambda own, number: assign_block(jax.random.fold_in(arg_keys[1], 2), own, number, TOK_DEV, EXPERTS, TOP, CAP, 2))(expert_ids_keys, expert_ids_turns).reshape((TOKENS, TOP))
    routing_gates = jnp.clip(jnp.exp(math.log(1.0) - 2.3025851 * jax.random.uniform(arg_keys[2], (TOKENS, TOP), jnp.float32) ** block_levels(arg_keys[2], (TOKENS, TOP), ((0, 16),), -0.2, 0.2)), 0.1, 1.0)
    w_gate = bell_draw(arg_keys[3], (EXPERTS, D, FF), D ** -0.5, 0.09375, ((0, 16), (2, 2)))
    w_up = bell_draw(arg_keys[4], (EXPERTS, D, FF), D ** -0.5, 0.09375, ((0, 16), (2, 2)))
    w_down = bell_draw(arg_keys[5], (EXPERTS, FF, D), FF ** -0.5, 0.1875, ((0, 16), (1, 2)))
    return {"tokens": tokens, "expert_ids": expert_ids, "routing_gates": routing_gates, "w_gate": w_gate, "w_up": w_up, "w_down": w_down}


def reference(tokens, expert_ids, routing_gates, w_gate, w_up, w_down):
    total_rows = TOKENS * TOP
    flat_ids = expert_ids.reshape(-1).astype(jnp.int32)
    blocks = flat_ids.reshape(N_EP, TOK_DEV * TOP)
    onehot = (blocks[:, :, None] == jnp.arange(EXPERTS, dtype=jnp.int32)[None, None, :]).astype(jnp.int32)
    row_ranks = jnp.sum((jnp.cumsum(onehot, axis=1) - 1) * onehot, axis=2).reshape(-1)
    sources = jnp.arange(total_rows, dtype=jnp.int32) // (TOK_DEV * TOP)
    position = flat_ids * (N_EP * CAP) + sources * CAP + row_ranks
    token_of = jnp.arange(total_rows, dtype=jnp.int32) // TOP
    slots_all = EXPERTS * N_EP * CAP
    row_table = jnp.full((slots_all,), TOKENS, jnp.int32).at[position].set(token_of).reshape(EXPERTS, N_EP * CAP)
    gate_table = jnp.zeros((slots_all,), jnp.float32).at[position].set(routing_gates.reshape(-1).astype(jnp.float32)).reshape(EXPERTS, N_EP * CAP)
    padded = jnp.concatenate([tokens, jnp.zeros((1, D), tokens.dtype)], axis=0)
    width_part = FF // N_ETP

    def expert_step(accum_rows, inputs):
        gate_mat, up_mat, down_mat, rows_index, gate_column = inputs
        inputs_rows = padded[rows_index]
        gate_val = jnp.dot(inputs_rows, gate_mat, preferred_element_type=jnp.float32)
        up_val = jnp.dot(inputs_rows, up_mat, preferred_element_type=jnp.float32)
        hidden = (jax.nn.silu(gate_val) * up_val).astype(jnp.bfloat16)
        summed = jnp.zeros((N_EP * CAP, D), jnp.float32)
        for part_index in range(N_ETP):
            lower = part_index * width_part
            partial_value = jnp.dot(hidden[:, lower:lower + width_part], down_mat[lower:lower + width_part], preferred_element_type=jnp.float32)
            rounded = lax.optimization_barrier(partial_value.astype(jnp.bfloat16))
            summed = summed + rounded.astype(jnp.float32)
        expert_out = summed.astype(jnp.bfloat16)
        contrib = gate_column[:, None] * expert_out.astype(jnp.float32)
        return accum_rows.at[rows_index].add(contrib), None

    start_rows = jnp.zeros((TOKENS + 1, D), jnp.float32)
    result, _ = lax.scan(expert_step, start_rows, (w_gate, w_up, w_down, row_table, gate_table))
    return result[:TOKENS].astype(jnp.bfloat16)
```

```python
import functools

import jax
import jax.numpy as jnp
from jax import lax
from jax.experimental import pallas as pl
from jax.experimental.pallas import tpu as pltpu
from jax.sharding import PartitionSpec as P

MESH = pl.DeviceIdType.MESH
F32 = jnp.float32
PLANES = 4
SIDE = 4


def plain_shards(tokens, expert_ids, routing_gates, w_gate, w_up, w_down):
    ep_count = lax.axis_size("ep")
    tok_rows, topk_count = expert_ids.shape
    model_width = tokens.shape[1]
    half_width = model_width // lax.axis_size("etp")
    capacity = max(2, tok_rows * topk_count * 9 // (8 * ep_count))
    flat_ids = expert_ids.reshape(-1)
    onehot = (flat_ids[:, None] == jnp.arange(ep_count, dtype=jnp.int32)[None, :]).astype(jnp.bfloat16)
    row_range = jnp.arange(tok_rows * topk_count, dtype=jnp.int32)
    earlier = (row_range[None, :] < row_range[:, None]).astype(jnp.bfloat16)
    counted = jnp.dot(earlier, onehot, preferred_element_type=F32)
    row_ranks = jnp.sum(counted * onehot.astype(F32), axis=1).astype(jnp.int32)
    slot_index = flat_ids * capacity + row_ranks
    slot_table = slot_index.reshape(tok_rows, topk_count)
    slot_range = jnp.arange(ep_count * capacity, dtype=jnp.int32)
    dispatch = jnp.any(slot_range[:, None, None] == slot_table[None, :, :], axis=2).astype(
        jnp.bfloat16
    )
    outgoing = jnp.dot(dispatch, tokens, preferred_element_type=jnp.float32).astype(jnp.bfloat16)
    outgoing = outgoing.reshape(ep_count, capacity, model_width)
    arrived = lax.all_to_all(outgoing, "ep", split_axis=0, concat_axis=0, tiled=True)
    expert_rows = arrived.reshape(ep_count * capacity, model_width)
    gate_val = jnp.dot(expert_rows, w_gate[0], preferred_element_type=jnp.float32)
    up_val = jnp.dot(expert_rows, w_up[0], preferred_element_type=jnp.float32)
    hidden = (jax.nn.silu(gate_val) * up_val).astype(jnp.bfloat16)
    partial_value = jnp.dot(hidden, w_down[0], preferred_element_type=jnp.float32)
    summed = lax.psum_scatter(
        partial_value.astype(jnp.bfloat16), "etp", scatter_dimension=1, tiled=True
    )
    outgoing_back = summed.reshape(ep_count, capacity, half_width)
    returned = lax.all_to_all(outgoing_back, "ep", split_axis=0, concat_axis=0, tiled=True).reshape(
        -1, half_width
    )
    picked = returned[slot_index].reshape(tok_rows, topk_count, half_width).astype(jnp.float32)
    combined = jnp.einsum("tk,tkd->td", routing_gates, picked)
    return combined.astype(jnp.bfloat16)


def kernel(
    tok, wts, wg_h, wu_h, wd_h, out,
    xd, xc, sb, pk, wbuf, wg, wu, wd, hid, con, rb, dd, ra, rz,
    sem_l, s_z, r_z, s_a, r_a, s_b, r_b, s_c, r_c, s_h, r_h, s_d, r_d, s_w, r_w,
    s_rb, r_rb, s_ra, r_ra, s_rz, r_rz,
):
    me, c = lax.axis_index("ep"), lax.axis_index("etp")
    n = PLANES * SIDE
    oc = 1 - c
    x, y, z = me % 2, (me // 2) % 2, me // 4
    j = me % 4
    xj, yj = j + 1 - 2 * x, j + 2 - 4 * y
    ja = xj + c * (yj - xj)
    jb = yj + c * (xj - yj)
    jd = xj + yj - j
    pa, pb = me - j + ja, me - j + jb
    ga, gb, gd = 1 + c, 2 - c, 3
    z1, z2, z3 = z + 1 - 2 * (z % 2), z + 2 - 4 * (z // 2), 3 - z
    mid = (z % 2 + z // 2) % 2
    zs = [z, z1, z2 + mid * (z3 - z2), z3 + mid * (z2 - z3)]
    zq = [0, 1, 3 - mid, 3 - mid]
    rows, half = out.shape
    width = wg.shape[1]
    cap = sb.shape[2]
    bf = jnp.bfloat16

    def rdma(src, dst, ss, rs, ep, core):
        return pltpu.make_async_remote_copy(
            src_ref=src, dst_ref=dst, send_sem=ss, recv_sem=rs,
            device_id=(ep, core), device_id_type=MESH,
        )

    barrier = pltpu.get_barrier_semaphore()
    for d in range(1, n):
        pl.semaphore_signal(barrier, inc=1, device_id=((me + d) % n, c), device_id_type=MESH)
    pl.semaphore_signal(barrier, inc=1, device_id=(me, oc), device_id_type=MESH)

    def cols(k):
        return pl.ds(pl.multiple_of(k * half, 128), half)

    loc = [
        pltpu.make_async_copy(tok.at[:, cols(c)], xd.at[0, 0], sem_l.at[0]),
        pltpu.make_async_copy(wts, wbuf.at[me], sem_l.at[1]),
        pltpu.make_async_copy(wg_h.at[0], wg, sem_l.at[2]),
        pltpu.make_async_copy(wu_h.at[0], wu, sem_l.at[3]),
        pltpu.make_async_copy(wd_h.at[0, :, cols(c)], wd.at[c], sem_l.at[4]),
    ]
    for cp in loc:
        cp.start()
    pl.semaphore_wait(barrier, n)
    loc[0].wait()

    def send_z(k):
        return rdma(xd.at[0, 0], xd.at[k, 0], s_z.at[k - 1], r_z.at[k - 1], (z1 if k == 1 else z3) * SIDE + j, c)

    def pass_z(k):
        to, slot = ((z3, 3), (z1, 2), (z1, 3))[k - 1]
        return rdma(xd.at[k, 0], xd.at[slot, 0], s_z.at[1 + k], r_z.at[slot - 1], to * SIDE + j, c)

    def send_a(k):
        return rdma(xd.at[k, 0], xd.at[k, 1], s_a.at[k], r_a.at[k], pa, c)

    def send_b(k, i):
        return rdma(
            sb.at[k, i], xc.at[c, k, gb if i == 0 else gd], s_b.at[k, i], r_b.at[k, i], pb, c
        )

    def send_c(k, g):
        blk = xc.at[c, k, g]
        return rdma(blk, blk, s_c.at[k, g], r_c.at[k, g], me, oc)

    def send_w(k, role):
        blk = wbuf.at[me]
        jj = [j, ja, jb, jd][role]
        return rdma(blk, blk, s_w.at[k, role], r_w.at[zq[k], role], zs[k] * SIDE + jj, c)

    def wait_w(k, role):
        blk = wbuf.at[me]
        rdma(blk, blk, s_w.at[k, role], r_w.at[k, role], pa, c).wait_recv()

    w_pairs = [(k, role) for k in range(PLANES) for role in range(4) if (k, role) != (0, 0)]
    send_d = rdma(wd_h.at[0, :, cols(oc)], wd.at[c], s_d, r_d, me, oc)

    def picks(k, jj, experts):
        w = wbuf[zs[k] * SIDE + jj]
        routed = jnp.where(w > 0.0, 1.0, 0.0)
        before = lax.broadcasted_iota(jnp.int32, (rows, rows), 0) < lax.broadcasted_iota(
            jnp.int32, (rows, rows), 1
        )
        rank = jnp.dot(
            routed.astype(bf), jnp.where(before, 1.0, 0.0).astype(bf), preferred_element_type=F32
        )
        row_of = lax.broadcasted_iota(jnp.int32, (n, rows), 0)
        slot = lax.broadcasted_iota(jnp.int32, (cap, rows), 0).astype(F32)
        result = []
        for e in experts:
            keep = row_of == e
            place = jnp.sum(jnp.where(keep, jnp.where(w > 0.0, rank, -1.0), 0.0), axis=0, keepdims=True)
            gate = jnp.sum(jnp.where(keep, w, 0.0), axis=0, keepdims=True)
            result.append((slot == place, gate))
        return result

    def compact(k, i):
        mine, theirs = picks(k, j if i == 0 else ja, (me, pb))
        both = [jnp.where(p[0], 1.0, 0.0).astype(bf) for p in (mine, theirs)]
        pk[k, i, 0] = both[0]
        pk[k, i, 1] = both[1]
        g = 0 if i == 0 else ga
        tile = 256

        @pl.loop(0, half // tile)
        def _(t):
            at = pl.ds(pl.multiple_of(t * tile, tile), tile)
            blk = xd[k, i, :, at]
            sb[k, i, :, at] = jnp.dot(both[1], blk, preferred_element_type=F32).astype(bf)
            xc[c, k, g, :, at] = jnp.dot(both[0], blk, preferred_element_type=F32).astype(bf)

        send_b(k, i).start()
        send_c(k, g).start()

    def stage1(k):
        if k > 0:
            send_z(k).wait_recv()
            pl.when(mid == 1)(pass_z(k).start)
        send_a(k).start()
        if k > 0:
            wait_w(k, 0)
        compact(k, 0)

    def stage2(k):
        send_a(k).wait_recv()
        wait_w(k, 1)
        compact(k, 1)

    def stage3(k):
        send_b(k, 0).wait_recv()
        send_c(k, gb).start()
        send_b(k, 1).wait_recv()
        send_c(k, gd).start()

    def stage4(k):
        for g in range(4):
            send_c(k, g).wait_recv()

    def hidden_up(k):
        tile = min(256, width)

        @pl.loop(0, width // tile)
        def _(t):
            at = pl.ds(pl.multiple_of(t * tile, tile), tile)
            x0 = xc[0, k].reshape(SIDE * cap, half)
            x1 = xc[1, k].reshape(SIDE * cap, half)
            g = jnp.dot(x0, wg[:half, at], preferred_element_type=F32)
            g = g + jnp.dot(x1, wg[half:, at], preferred_element_type=F32)
            u = jnp.dot(x0, wu[:half, at], preferred_element_type=F32)
            u = u + jnp.dot(x1, wu[half:, at], preferred_element_type=F32)
            hid[k, c, :, at] = (g / (1.0 + jnp.exp(-g)) * u).astype(bf)

    def send_h(k):
        blk = hid.at[k, c]
        return rdma(blk, blk, s_h.at[k], r_h.at[k], me, oc)

    def down(k):
        scale = []
        for jj in (j, xj, yj, jd):
            ((pick, gate),) = picks(k, jj, (me,))
            scale.append(jnp.sum(jnp.where(pick, gate, 0.0), axis=1, keepdims=True))
        scale = jnp.concatenate(scale, axis=0)
        tile = 256

        @pl.loop(0, half // tile)
        def _(t):
            at = pl.ds(pl.multiple_of(t * tile, tile), tile)
            o = jnp.dot(hid[k, 0], wd[0, :, at], preferred_element_type=F32)
            o = o + jnp.dot(hid[k, 1], wd[1, :, at], preferred_element_type=F32)
            con[k, :, :, at] = (o * scale).reshape(SIDE, cap, tile).astype(bf)

    def ret_b(k, i):
        return rdma(con.at[k, gb if i == 0 else gd], rb.at[k, i], s_rb.at[k, i], r_rb.at[k, i], pb, c)

    def ret_a(k):
        return rdma(dd.at[k, 1], ra.at[k], s_ra.at[k], r_ra.at[k], pa, c)

    def ret_z(k):
        return rdma(dd.at[k, 0], rz.at[zq[k] - 1], s_rz.at[k - 1], r_rz.at[zq[k] - 1], zs[k] * SIDE + j, c)

    def landed_z(k):
        return rdma(dd.at[k, 0], rz.at[k - 1], s_rz.at[k - 1], r_rz.at[k - 1], zs[k] * SIDE + j, c)

    def expand(k, i):
        g = 0 if i == 0 else ga
        tile = 256
        dims = (((0,), (0,)), ((), ()))

        @pl.loop(0, half // tile)
        def _(t):
            at = pl.ds(pl.multiple_of(t * tile, tile), tile)
            o = lax.dot_general(pk[k, i, 0], con[k, g, :, at], dims, preferred_element_type=F32)
            o = o + lax.dot_general(pk[k, i, 1], rb[k, i, :, at], dims, preferred_element_type=F32)
            dd[k, i, :, at] = o.astype(bf)

    def back1(k):
        ret_b(k, 1).start()
        ret_b(k, 0).start()

    def back2(k):
        ret_b(k, 1).wait_recv()
        expand(k, 1)
        ret_a(k).start()
        ret_b(k, 0).wait_recv()
        expand(k, 0)

    def back3(k):
        ret_a(k).wait_recv()
        dd[k, 0] = (dd[k, 0].astype(F32) + ra[k].astype(F32)).astype(bf)
        if k > 0:
            ret_z(k).start()

    send_a(0).start()
    send_z(1).start()
    pl.when(mid == 1)(send_z(2).start)
    loc[1].wait()
    for k, role in w_pairs:
        send_w(k, role).start()
    compact(0, 0)
    send_d.start()
    first = []

    def ffn(k):
        stage4(k)
        if not first:
            loc[2].wait()
            loc[3].wait()
        hidden_up(k)
        send_h(k).start()
        if not first:
            loc[4].wait()
            send_d.wait_recv()
        first.append(k)
        wait_w(k, 2)
        wait_w(k, 3)
        send_h(k).wait_recv()
        down(k)
        back1(k)

    plan = (
        (stage2, 0), (stage1, 1), (stage3, 0), (stage2, 1), (stage1, 2), (stage3, 1),
        (stage2, 2), (stage1, 3), (ffn, 1), (stage3, 2), (stage2, 3), (ffn, 2),
        (back2, 1), (stage3, 3), (ffn, 3), (back2, 2), (back3, 1), (ffn, 0),
        (back2, 3), (back3, 2), (back3, 3), (back2, 0), (back3, 0),
    )
    for step, k in plan:
        step(k)
    total = dd[0, 0].astype(F32)
    for k in range(1, PLANES):
        landed_z(k).wait_recv()
        total = total + rz[k - 1].astype(F32)
    out[...] = total.astype(bf)

    send_d.wait_send()
    for k, role in w_pairs:
        send_w(k, role).wait_send()
    for k in range(PLANES):
        send_a(k).wait_send()
        for g in range(4):
            send_c(k, g).wait_send()
        send_h(k).wait_send()
        for i in range(2):
            send_b(k, i).wait_send()
            ret_b(k, i).wait_send()
        ret_a(k).wait_send()
        if k > 0:
            ret_z(k).wait_send()
    send_z(1).wait_send()

    @pl.when(mid == 1)
    def _():
        send_z(2).wait_send()
        for k in range(1, PLANES):
            pass_z(k).wait_send()


def plane_shards(tokens, expert_ids, routing_gates, w_gate, w_up, w_down):
    n = PLANES * SIDE
    rows, model_width = tokens.shape
    half = model_width // 2
    width = w_gate.shape[2]
    cap = rows * expert_ids.shape[1] * 9 // (8 * n)
    experts = jnp.arange(n, dtype=jnp.int32)
    weights = jnp.sum(
        jnp.where(expert_ids.T[None, :, :] == experts[:, None, None], routing_gates.T[None], 0.0), axis=1
    )
    bf = jnp.bfloat16
    dma = pltpu.SemaphoreType.DMA
    anyspec = pl.BlockSpec(memory_space=pl.ANY)
    return pl.pallas_call(
        kernel,
        out_shape=jax.ShapeDtypeStruct((rows, half), bf),
        in_specs=[anyspec] * 5,
        out_specs=pl.BlockSpec(memory_space=pltpu.VMEM),
        scratch_shapes=[
            pltpu.VMEM((PLANES, 2, rows, half), bf),
            pltpu.VMEM((2, PLANES, SIDE, cap, half), bf),
            pltpu.VMEM((PLANES, 2, cap, half), bf),
            pltpu.VMEM((PLANES, 2, 2, cap, rows), bf),
            pltpu.VMEM((n, n, rows), F32),
            pltpu.VMEM((model_width, width), bf),
            pltpu.VMEM((model_width, width), bf),
            pltpu.VMEM((2, width, half), bf),
            pltpu.VMEM((PLANES, 2, SIDE * cap, width), bf),
            pltpu.VMEM((PLANES, SIDE, cap, half), bf),
            pltpu.VMEM((PLANES, 2, cap, half), bf),
            pltpu.VMEM((PLANES, 2, rows, half), bf),
            pltpu.VMEM((PLANES, rows, half), bf),
            pltpu.VMEM((PLANES - 1, rows, half), bf),
            dma((5,)),
            dma((5,)), dma((3,)),
            dma((4,)), dma((4,)),
            dma((4, 2)), dma((4, 2)),
            dma((4, 4)), dma((4, 4)),
            dma((4,)), dma((4,)),
            dma, dma,
            dma((4, 4)), dma((4, 4)),
            dma((4, 2)), dma((4, 2)),
            dma((4,)), dma((4,)),
            dma((3,)), dma((3,)),
        ],
        compiler_params=pltpu.CompilerParams(
            collective_id=0, has_side_effects=True, vmem_limit_bytes=60 << 20
        ),
        cost_estimate=pl.CostEstimate(
            flops=6 * n * cap * model_width * width, bytes_accessed=12 << 20,
            transcendentals=n * cap * width,
        ),
        name="planes",
    )(tokens, weights, w_gate, w_up, w_down)


def solution(mesh):
    small = mesh.shape["ep"] == PLANES * SIDE and mesh.shape["etp"] == 2
    return jax.shard_map(
        plane_shards if small else plain_shards,
        mesh=mesh,
        in_specs=(
            P("ep", None),
            P("ep", None),
            P("ep", None),
            P("ep", None, "etp"),
            P("ep", None, "etp"),
            P("ep", "etp", None),
        ),
        out_specs=P("ep", "etp"),
        check_vma=False,
    )
```

```python
import functools

import jax
import jax.numpy as jnp
from jax import lax
from jax.experimental import pallas as pl
from jax.experimental.pallas import tpu as pltpu
from jax.sharding import PartitionSpec as P

MESH = pl.DeviceIdType.MESH
F32 = jnp.float32
PLANES = 4
SIDE = 4
PARTS = 2
END, MID = "end", "mid"
FETCH = {END: {1: "aa", 2: "aa", 3: "aa"}, MID: {1: "zz", 2: "zz", 3: "aa"}}
GIVE = {END: {1: "aa", 2: "zz", 3: "aa"}, MID: {1: "zz", 2: "aa", 3: "aa"}}
LANDING = {(1, 0): 0, (1, 2): 1, (1, 3): 2, (3, 0): 3, (3, 1): 4}


def plain_shards(tokens, expert_ids, routing_gates, w_gate, w_up, w_down):
    ep_count = lax.axis_size("ep")
    tok_rows, topk_count = expert_ids.shape
    model_width = tokens.shape[1]
    half_width = model_width // lax.axis_size("etp")
    capacity = max(2, tok_rows * topk_count * 9 // (8 * ep_count))
    flat_ids = expert_ids.reshape(-1)
    onehot = (flat_ids[:, None] == jnp.arange(ep_count, dtype=jnp.int32)[None, :]).astype(jnp.bfloat16)
    row_range = jnp.arange(tok_rows * topk_count, dtype=jnp.int32)
    earlier = (row_range[None, :] < row_range[:, None]).astype(jnp.bfloat16)
    counted = jnp.dot(earlier, onehot, preferred_element_type=F32)
    row_ranks = jnp.sum(counted * onehot.astype(F32), axis=1).astype(jnp.int32)
    slot_index = flat_ids * capacity + row_ranks
    slot_table = slot_index.reshape(tok_rows, topk_count)
    slot_range = jnp.arange(ep_count * capacity, dtype=jnp.int32)
    dispatch = jnp.any(slot_range[:, None, None] == slot_table[None, :, :], axis=2).astype(
        jnp.bfloat16
    )
    outgoing = jnp.dot(dispatch, tokens, preferred_element_type=jnp.float32).astype(jnp.bfloat16)
    outgoing = outgoing.reshape(ep_count, capacity, model_width)
    arrived = lax.all_to_all(outgoing, "ep", split_axis=0, concat_axis=0, tiled=True)
    expert_rows = arrived.reshape(ep_count * capacity, model_width)
    gate_val = jnp.dot(expert_rows, w_gate[0], preferred_element_type=jnp.float32)
    up_val = jnp.dot(expert_rows, w_up[0], preferred_element_type=jnp.float32)
    hidden = (jax.nn.silu(gate_val) * up_val).astype(jnp.bfloat16)
    partial_value = jnp.dot(hidden, w_down[0], preferred_element_type=jnp.float32)
    summed = lax.psum_scatter(
        partial_value.astype(jnp.bfloat16), "etp", scatter_dimension=1, tiled=True
    )
    outgoing_back = summed.reshape(ep_count, capacity, half_width)
    returned = lax.all_to_all(outgoing_back, "ep", split_axis=0, concat_axis=0, tiled=True).reshape(
        -1, half_width
    )
    picked = returned[slot_index].reshape(tok_rows, topk_count, half_width).astype(jnp.float32)
    combined = jnp.einsum("tk,tkd->td", routing_gates, picked)
    return combined.astype(jnp.bfloat16)


def kernel(
    tok, wts, wg_h, wu_h, wd_h, out,
    xd, xc, sb, pk, pt, gc, wbuf, wg, wu, wd, hid, con, rb, dd, ra, rz,
    sem_l, s_z, s_al, r_x, s_b, r_b, s_c, r_c, s_h, r_h, s_d, r_d, s_w, r_w,
    s_rb, r_rb, s_ra, r_ra, s_rz, r_rz,
):
    me, c = lax.axis_index("ep"), lax.axis_index("etp")
    n = PLANES * SIDE
    oc = 1 - c
    x, y, z = me % 2, (me // 2) % 2, me // 4
    j = me % 4
    xj, yj = j + 1 - 2 * x, j + 2 - 4 * y
    ja = xj + c * (yj - xj)
    jb = yj + c * (xj - yj)
    pa, pb = me - j + ja, me - j + jb
    ga, gb, gd = 1 + c, 2 - c, 3
    z1, z2, z3 = z + 1 - 2 * (z % 2), z + 2 - 4 * (z // 2), 3 - z
    zs = [z, z1, z2, z3]
    mid = (z % 2 + z // 2) % 2
    rows, half = out.shape
    width = wg.shape[1]
    cap = sb.shape[2]
    bf = jnp.bfloat16
    tile = 256
    tiles = half // tile
    cuts = [(p * tiles + PARTS - 1) // PARTS for p in range(PARTS + 1)]
    parts = range(PARTS)

    def span(h):
        return pl.ds(cuts[h] * tile, (cuts[h + 1] - cuts[h]) * tile)

    def rdma(src, dst, ss, rs, ep, core):
        return pltpu.make_async_remote_copy(
            src_ref=src, dst_ref=dst, send_sem=ss, recv_sem=rs,
            device_id=(ep, core), device_id_type=MESH,
        )

    barrier = pltpu.get_barrier_semaphore()
    for d in range(1, n):
        pl.semaphore_signal(barrier, inc=1, device_id=((me + d) % n, c), device_id_type=MESH)
    pl.semaphore_signal(barrier, inc=1, device_id=(me, oc), device_id_type=MESH)

    def cols(k):
        return pl.ds(pl.multiple_of(k * half, 128), half)

    loc = [
        pltpu.make_async_copy(tok.at[:, cols(c)], xd.at[0, 0], sem_l.at[0]),
        pltpu.make_async_copy(wts, wbuf.at[0, 0], sem_l.at[1]),
        pltpu.make_async_copy(wg_h.at[0], wg, sem_l.at[2]),
        pltpu.make_async_copy(wu_h.at[0], wu, sem_l.at[3]),
        pltpu.make_async_copy(wd_h.at[0, :, cols(c)], wd.at[c], sem_l.at[4]),
    ]
    for cp in loc:
        cp.start()
    pl.semaphore_wait(barrier, n)
    loc[0].wait()

    def send_z(nb, k, i, h):
        blk = xd.at[k, i, :, span(h)]
        dst = xd.at[k ^ nb, i, :, span(h)]
        return rdma(blk, dst, s_z.at[nb // 2, k, i, h], r_x.at[k ^ nb, i, h], zs[nb] * SIDE + j, c)

    def send_al(k, h):
        return rdma(
            xd.at[k, 0, :, span(h)], xd.at[k, 1, :, span(h)], s_al.at[k, h], r_x.at[k, 1, h], pa, c
        )

    def landed(k, i, h):
        blk = xd.at[k, i, :, span(h)]
        return rdma(blk, blk, s_al.at[k, h], r_x.at[k, i, h], pa, c)

    def send_b(k, i, h):
        return rdma(
            sb.at[k, i, :, span(h)], xc.at[c, k, gb if i == 0 else gd, :, span(h)],
            s_b.at[k, i, h], r_b.at[k, i, h], pb, c,
        )

    def send_c(k, g):
        blk = xc.at[c, k, g]
        return rdma(blk, blk, s_c.at[k, g], r_c.at[k, g], me, oc)

    def send_w(k, i):
        to = zs[k] * SIDE + (j if i == 0 else ja)
        return rdma(wbuf.at[0, 0], wbuf.at[k, i], s_w.at[k, i], r_w.at[k, i], to, c)

    w_pairs = [(k, i) for i in (1, 0) for k in range(PLANES) if (k, i) != (0, 0)]
    send_d = rdma(wd_h.at[0, :, cols(oc)], wd.at[c], s_d, r_d, me, oc)

    def send_h(k):
        blk = hid.at[k, c]
        return rdma(blk, blk, s_h.at[k], r_h.at[k], me, oc)

    def ret_b(k, i, h):
        return rdma(
            con.at[k, gb if i == 0 else gd, :, span(h)], rb.at[k, i, :, span(h)],
            s_rb.at[k, i, h], r_rb.at[k, i, h], pb, c,
        )

    def ret_a(k, h):
        return rdma(
            dd.at[k, 1, :, span(h)], ra.at[k, :, span(h)], s_ra.at[k, h], r_ra.at[k, h], pa, c
        )

    def ret_z(nb, k, i, h):
        slot = LANDING[nb, k ^ nb]
        return rdma(
            dd.at[k, i, :, span(h)], rz.at[slot, i, :, span(h)],
            s_rz.at[k, i, h], r_rz.at[slot, i, h], zs[nb] * SIDE + j, c,
        )

    def summed(slot, i, h):
        blk = rz.at[slot, i, :, span(h)]
        return rdma(blk, blk, s_rz.at[0, i, h], r_rz.at[slot, i, h], pa, c)

    def place(k, i):
        w = wbuf[k, i]
        routed = jnp.where(w > 0.0, 1.0, 0.0)
        first = lax.broadcasted_iota(jnp.int32, (rows, rows), 0)
        second = lax.broadcasted_iota(jnp.int32, (rows, rows), 1)
        rank = jnp.dot(
            routed.astype(bf), jnp.where(first < second, 1.0, 0.0).astype(bf),
            preferred_element_type=F32,
        )
        rank = jnp.where(w > 0.0, rank, -1.0)
        row_of = lax.broadcasted_iota(jnp.int32, (n, rows), 0)
        slot = lax.broadcasted_iota(jnp.int32, (cap, rows), 0).astype(F32)
        slot_t = lax.broadcasted_iota(jnp.int32, (rows, cap), 1).astype(F32)
        picked = []
        for q, e in enumerate((me, pb)):
            keep = row_of == e
            at = jnp.sum(jnp.where(keep, rank, 0.0), axis=0, keepdims=True)
            gate = jnp.sum(jnp.where(keep, w, 0.0), axis=0, keepdims=True)
            picked.append(jnp.where(slot == at, 1.0, 0.0))
            at_t = jnp.sum(jnp.where(first == second, at, 0.0), axis=1, keepdims=True)
            gate_t = jnp.sum(jnp.where(first == second, gate, 0.0), axis=1, keepdims=True)
            pt[k, i, q] = jnp.where(slot_t == at_t, 1.0, 0.0).astype(bf)
            gc[k, i, q] = jnp.broadcast_to(gate_t, (rows, 128))
        pk[k, i] = jnp.concatenate(picked, axis=0).astype(bf)

    class Role:
        def __init__(self, name):
            self.name = name
            self.other = {1: MID if name == END else END, 3: MID}
            self.nbs = (1,) if name == END else (1, 3)
            self.seen = set()

        def once(self, key, copy):
            if key not in self.seen:
                self.seen.add(key)
                copy.wait_recv()

        def forwards(self, k, i, h):
            found = []
            for nb in self.nbs:
                to = k ^ nb
                if to == 0 or (self.other[nb] == MID and nb == 1 and k != 0):
                    continue
                if nb == 3 and k not in (0, 1) or nb == 1 and self.name == MID and k == 1:
                    continue
                if i == 0 or FETCH[self.other[nb]][to][h] == "z":
                    found.append(nb)
            return found

        def along(self, k, h):
            return k == 0 or FETCH[self.name][k][h] == "a"

        def beside(self, k, h):
            return k == 0 or GIVE[self.name][k][h] == "a"

        def get(self, k, i, h):
            if (k, i, h) in self.seen:
                return
            self.seen.add((k, i, h))
            if (k, i) != (0, 0):
                landed(k, i, h).wait_recv()
            for nb in self.forwards(k, i, h):
                send_z(nb, k, i, h).start()
            if i == 0 and self.along(k, h):
                send_al(k, h).start()

        def compact(self, k, i):
            if (k, i) != (0, 0):
                self.once(("w", k, i), send_w(k, i))
            place(k, i)
            g = 0 if i == 0 else ga
            for h in parts:
                self.get(k, i, h)
                at = span(h)
                o = jnp.dot(pk[k, i], xd[k, i, :, at], preferred_element_type=F32)
                xc[c, k, g, :, at] = o[:cap].astype(bf)
                sb[k, i, :, at] = o[cap:].astype(bf)
                send_b(k, i, h).start()
            send_c(k, g).start()

        def relay(self, k, i):
            for h in parts:
                self.once(("b", k, i, h), send_b(k, i, h))
            send_c(k, gb if i == 0 else gd).start()

        def up(self, k):
            if "up" not in self.seen:
                self.seen.add("up")
                loc[2].wait()
                loc[3].wait()
            for g in range(4):
                self.once(("c", k, g), send_c(k, g))
            step = min(256, width)

            @pl.loop(0, width // step)
            def _(t):
                at = pl.ds(pl.multiple_of(t * step, step), step)
                x0 = xc[0, k].reshape(SIDE * cap, half)
                x1 = xc[1, k].reshape(SIDE * cap, half)
                g = jnp.dot(x0, wg[:half, at], preferred_element_type=F32)
                g = g + jnp.dot(x1, wg[half:, at], preferred_element_type=F32)
                u = jnp.dot(x0, wu[:half, at], preferred_element_type=F32)
                u = u + jnp.dot(x1, wu[half:, at], preferred_element_type=F32)
                hid[k, c, :, at] = (g / (1.0 + jnp.exp(-g)) * u).astype(bf)

            send_h(k).start()

        def down(self, k):
            if "down" not in self.seen:
                self.seen.add("down")
                loc[4].wait()
                send_d.wait_recv()
            self.once(("h", k), send_h(k))

            for h in parts:
                at = span(h)
                o = jnp.dot(hid[k, 0], wd[0, :, at], preferred_element_type=F32)
                o = o + jnp.dot(hid[k, 1], wd[1, :, at], preferred_element_type=F32)
                con[k, :, :, at] = o.reshape(SIDE, cap, at.size).astype(bf)

        def give(self, k, i):
            for h in parts:
                ret_b(k, i, h).start()

        def incoming(self, k, i, h):
            slots = []
            for nb in self.nbs:
                if (nb, k) in LANDING and not (self.name == END and k != 0):
                    if i == 0 or GIVE[self.other[nb]][k ^ nb][h] == "z":
                        slots.append(LANDING[nb, k])
            return slots

        def toward(self, k):
            return 1 if self.name == END or k == 1 else 3

        def back(self, k, i, h):
            g = 0 if i == 0 else ga
            slots = self.incoming(k, i, h)
            ret_b(k, i, h).wait_recv()
            for s in slots:
                summed(s, i, h).wait_recv()
            if i == 0 and self.beside(k, h):
                ret_a(k, h).wait_recv()
            at = span(h)
            o = jnp.dot(pt[k, i, 0], con[k, g, :, at], preferred_element_type=F32) * gc[k, i, 0, :, 0:1]
            p = jnp.dot(pt[k, i, 1], rb[k, i, :, at], preferred_element_type=F32) * gc[k, i, 1, :, 0:1]
            o = o + p
            for s in slots:
                o = o + rz[s, i, :, at].astype(F32)
            if i == 0 and self.beside(k, h):
                o = o + ra[k, :, at].astype(F32)
            if (k, i) == (0, 0):
                out[:, at] = o.astype(bf)
                return
            dd[k, i, :, at] = o.astype(bf)
            if i == 1 and self.beside(k, h):
                ret_a(k, h).start()
            else:
                ret_z(self.toward(k), k, i, h).start()

        def finish(self):
            send_d.wait_send()
            for k, i in w_pairs:
                send_w(k, i).wait_send()
            for k in range(PLANES):
                for g in range(4):
                    send_c(k, g).wait_send()
                send_h(k).wait_send()
                for h in parts:
                    if self.along(k, h):
                        send_al(k, h).wait_send()
                    if self.beside(k, h):
                        ret_a(k, h).wait_send()
                    for i in range(2):
                        for nb in self.forwards(k, i, h):
                            send_z(nb, k, i, h).wait_send()
                        send_b(k, i, h).wait_send()
                        ret_b(k, i, h).wait_send()
                        if k > 0 and (i == 0 or not self.beside(k, h)):
                            ret_z(self.toward(k), k, i, h).wait_send()

        def run(self, plan):
            for h in parts:
                self.get(0, 0, h)
            loc[1].wait()
            for k, i in w_pairs:
                send_w(k, i).start()
            self.compact(0, 0)
            send_d.start()
            for what, *at in plan:
                getattr(self, what)(*at)
            self.finish()

    @pl.when(mid == 0)
    def _():
        Role(END).run(PLAN[END])

    @pl.when(mid == 1)
    def _():
        Role(MID).run(PLAN[MID])


PLAN = {
    END: (
        ("compact", 1, 0), ("compact", 0, 1), ("compact", 2, 0), ("compact", 2, 1),
        ("relay", 2, 0), ("relay", 1, 0), ("compact", 3, 0), ("relay", 2, 1),
        ("up", 2), ("compact", 3, 1), ("compact", 1, 1), ("relay", 3, 0),
        ("down", 2), ("relay", 3, 1), ("give", 2, 1), ("give", 2, 0),
        ("up", 3), ("relay", 1, 1), ("back", 2, 1, 1), ("back", 2, 1, 0),
        ("down", 3), ("relay", 0, 1), ("relay", 0, 0), ("give", 3, 1),
        ("give", 3, 0), ("back", 2, 0, 1), ("up", 1), ("back", 3, 1, 0),
        ("get", 0, 1, 0), ("up", 0), ("back", 3, 0, 0), ("back", 3, 1, 1),
        ("down", 1), ("give", 1, 1), ("give", 1, 0), ("back", 3, 0, 1),
        ("down", 0), ("back", 2, 0, 0), ("give", 0, 1), ("back", 1, 1, 0),
        ("back", 1, 1, 1), ("get", 0, 1, 1), ("back", 0, 1, 0), ("back", 1, 0, 0),
        ("back", 0, 1, 1), ("give", 0, 0), ("back", 1, 0, 1), ("back", 0, 0, 0),
        ("back", 0, 0, 1),
    ),
    MID: (
        ("get", 3, 0, 0), ("get", 1, 0, 0), ("compact", 3, 0), ("compact", 0, 1),
        ("get", 1, 0, 1), ("compact", 3, 1), ("compact", 2, 0), ("compact", 1, 0),
        ("relay", 0, 1), ("compact", 1, 1), ("get", 3, 0, 1), ("relay", 3, 1),
        ("relay", 2, 0), ("relay", 0, 0), ("relay", 3, 0), ("up", 3),
        ("up", 0), ("relay", 1, 0), ("compact", 2, 1), ("relay", 1, 1),
        ("down", 3), ("give", 3, 0), ("up", 1), ("relay", 2, 1),
        ("down", 0), ("down", 1), ("give", 3, 1), ("give", 1, 1),
        ("give", 0, 1), ("up", 2), ("down", 2), ("get", 1, 1, 0),
        ("get", 0, 1, 1), ("back", 3, 1, 1), ("give", 2, 1), ("give", 0, 0),
        ("back", 2, 1, 0), ("back", 2, 1, 1), ("back", 1, 1, 0), ("back", 3, 0, 1),
        ("get", 2, 1, 0), ("get", 3, 1, 1), ("give", 2, 0), ("back", 0, 1, 1),
        ("back", 1, 1, 1), ("back", 3, 1, 0), ("give", 1, 0), ("get", 3, 1, 0),
        ("back", 2, 0, 0), ("get", 2, 0, 1), ("back", 2, 0, 1), ("back", 1, 0, 0),
        ("back", 3, 0, 0), ("back", 1, 0, 1), ("back", 0, 1, 0), ("get", 1, 1, 1),
        ("get", 2, 0, 0), ("get", 0, 1, 0), ("get", 2, 1, 1), ("back", 0, 0, 0),
        ("back", 0, 0, 1),
    ),
}


def plane_shards(tokens, expert_ids, routing_gates, w_gate, w_up, w_down):
    n = PLANES * SIDE
    rows, model_width = tokens.shape
    half = model_width // 2
    width = w_gate.shape[2]
    cap = rows * expert_ids.shape[1] * 9 // (8 * n)
    experts = jnp.arange(n, dtype=jnp.int32)
    weights = jnp.sum(
        jnp.where(expert_ids.T[None, :, :] == experts[:, None, None], routing_gates.T[None], 0.0), axis=1
    )
    bf = jnp.bfloat16
    dma = pltpu.SemaphoreType.DMA
    anyspec = pl.BlockSpec(memory_space=pl.ANY)
    return pl.pallas_call(
        kernel,
        out_shape=jax.ShapeDtypeStruct((rows, half), bf),
        in_specs=[anyspec] * 5,
        out_specs=pl.BlockSpec(memory_space=pltpu.VMEM),
        scratch_shapes=[
            pltpu.VMEM((PLANES, 2, rows, half), bf),
            pltpu.VMEM((2, PLANES, SIDE, cap, half), bf),
            pltpu.VMEM((PLANES, 2, cap, half), bf),
            pltpu.VMEM((PLANES, 2, 2 * cap, rows), bf),
            pltpu.VMEM((PLANES, 2, 2, rows, cap), bf),
            pltpu.VMEM((PLANES, 2, 2, rows, 128), F32),
            pltpu.VMEM((PLANES, 2, n, rows), F32),
            pltpu.VMEM((model_width, width), bf),
            pltpu.VMEM((model_width, width), bf),
            pltpu.VMEM((2, width, half), bf),
            pltpu.VMEM((PLANES, 2, SIDE * cap, width), bf),
            pltpu.VMEM((PLANES, SIDE, cap, half), bf),
            pltpu.VMEM((PLANES, 2, cap, half), bf),
            pltpu.VMEM((PLANES, 2, rows, half), bf),
            pltpu.VMEM((PLANES, rows, half), bf),
            pltpu.VMEM((len(LANDING), 2, rows, half), bf),
            dma((5,)),
            dma((2, PLANES, 2, PARTS)), dma((PLANES, PARTS)), dma((PLANES, 2, PARTS)),
            dma((PLANES, 2, PARTS)), dma((PLANES, 2, PARTS)),
            dma((PLANES, SIDE)), dma((PLANES, SIDE)),
            dma((PLANES,)), dma((PLANES,)),
            dma, dma,
            dma((PLANES, 2)), dma((PLANES, 2)),
            dma((PLANES, 2, PARTS)), dma((PLANES, 2, PARTS)),
            dma((PLANES, PARTS)), dma((PLANES, PARTS)),
            dma((PLANES, 2, PARTS)), dma((len(LANDING), 2, PARTS)),
        ],
        compiler_params=pltpu.CompilerParams(
            collective_id=0, has_side_effects=True, vmem_limit_bytes=60 << 20
        ),
        cost_estimate=pl.CostEstimate(
            flops=6 * n * cap * model_width * width, bytes_accessed=12 << 20,
            transcendentals=n * cap * width,
        ),
        name="planes",
    )(tokens, weights, w_gate, w_up, w_down)


def solution(mesh):
    small = mesh.shape["ep"] == PLANES * SIDE and mesh.shape["etp"] == 2
    return jax.shard_map(
        plane_shards if small else plain_shards,
        mesh=mesh,
        in_specs=(
            P("ep", None),
            P("ep", None),
            P("ep", None),
            P("ep", None, "etp"),
            P("ep", None, "etp"),
            P("ep", "etp", None),
        ),
        out_specs=P("ep", "etp"),
        check_vma=False,
    )
```

```python
import functools

import jax
import jax.numpy as jnp
from jax import lax
from jax.experimental import pallas as pl
from jax.experimental.pallas import tpu as pltpu
from jax.sharding import PartitionSpec as P

MESH = pl.DeviceIdType.MESH
F32 = jnp.float32
PLANES = 4
SIDE = 4
PARTS = 2
END, MID = "end", "mid"
FETCH = {END: {0: "aa", 1: "aa", 2: "az", 3: "az"}, MID: {0: "aa", 1: "az", 2: "za", 3: "aa"}}
GIVE = {END: {0: "aa", 1: "aa", 2: "aa", 3: "za"}, MID: {0: "aa", 1: "zz", 2: "zz", 3: "aa"}}
LANDING = {(1, 0): 0, (1, 2): 1, (1, 3): 2, (3, 0): 3, (3, 1): 4}


def plain_shards(tokens, expert_ids, routing_gates, w_gate, w_up, w_down):
    ep_count = lax.axis_size("ep")
    tok_rows, topk_count = expert_ids.shape
    model_width = tokens.shape[1]
    half_width = model_width // lax.axis_size("etp")
    capacity = max(2, tok_rows * topk_count * 9 // (8 * ep_count))
    flat_ids = expert_ids.reshape(-1)
    onehot = (flat_ids[:, None] == jnp.arange(ep_count, dtype=jnp.int32)[None, :]).astype(jnp.bfloat16)
    row_range = jnp.arange(tok_rows * topk_count, dtype=jnp.int32)
    earlier = (row_range[None, :] < row_range[:, None]).astype(jnp.bfloat16)
    counted = jnp.dot(earlier, onehot, preferred_element_type=F32)
    row_ranks = jnp.sum(counted * onehot.astype(F32), axis=1).astype(jnp.int32)
    slot_index = flat_ids * capacity + row_ranks
    slot_table = slot_index.reshape(tok_rows, topk_count)
    slot_range = jnp.arange(ep_count * capacity, dtype=jnp.int32)
    dispatch = jnp.any(slot_range[:, None, None] == slot_table[None, :, :], axis=2).astype(
        jnp.bfloat16
    )
    outgoing = jnp.dot(dispatch, tokens, preferred_element_type=jnp.float32).astype(jnp.bfloat16)
    outgoing = outgoing.reshape(ep_count, capacity, model_width)
    arrived = lax.all_to_all(outgoing, "ep", split_axis=0, concat_axis=0, tiled=True)
    expert_rows = arrived.reshape(ep_count * capacity, model_width)
    gate_val = jnp.dot(expert_rows, w_gate[0], preferred_element_type=jnp.float32)
    up_val = jnp.dot(expert_rows, w_up[0], preferred_element_type=jnp.float32)
    hidden = (jax.nn.silu(gate_val) * up_val).astype(jnp.bfloat16)
    partial_value = jnp.dot(hidden, w_down[0], preferred_element_type=jnp.float32)
    summed = lax.psum_scatter(
        partial_value.astype(jnp.bfloat16), "etp", scatter_dimension=1, tiled=True
    )
    outgoing_back = summed.reshape(ep_count, capacity, half_width)
    returned = lax.all_to_all(outgoing_back, "ep", split_axis=0, concat_axis=0, tiled=True).reshape(
        -1, half_width
    )
    picked = returned[slot_index].reshape(tok_rows, topk_count, half_width).astype(jnp.float32)
    combined = jnp.einsum("tk,tkd->td", routing_gates, picked)
    return combined.astype(jnp.bfloat16)


def kernel(
    tok, ids_h, gates_h, wg_h, wu_h, wd_h, out,
    xd, xc, sb, pk, pt, gc, ids, gates, wbuf, wg, wu, wd, hid, con, rb, dd, ra, rz,
    sem_l, s_z, s_al, r_x, s_b, r_b, s_c, r_c, s_h, r_h, s_d, r_d, s_w, r_w,
    s_rb, r_rb, s_ra, r_ra, s_rz, r_rz,
):
    me, c = lax.axis_index("ep"), lax.axis_index("etp")
    n = PLANES * SIDE
    oc = 1 - c
    x, y, z = me % 2, (me // 2) % 2, me // 4
    j = me % 4
    xj, yj = j + 1 - 2 * x, j + 2 - 4 * y
    ja = xj + c * (yj - xj)
    jb = yj + c * (xj - yj)
    pa, pb, pd = me - j + ja, me - j + jb, me - j + xj + yj - j
    ga, gb, gd = 1 + c, 2 - c, 3
    z1, z2, z3 = z + 1 - 2 * (z % 2), z + 2 - 4 * (z // 2), 3 - z
    zs = [z, z1, z2, z3]
    mid = (z % 2 + z // 2) % 2
    rows, half = out.shape
    width = wg.shape[1]
    cap = sb.shape[2]
    bf = jnp.bfloat16
    tile = 256
    tiles = half // tile
    cuts = [(p * tiles + PARTS - 1) // PARTS for p in range(PARTS + 1)]
    parts = range(PARTS)

    def span(h):
        return pl.ds(cuts[h] * tile, (cuts[h + 1] - cuts[h]) * tile)

    def rdma(src, dst, ss, rs, ep, core):
        return pltpu.make_async_remote_copy(
            src_ref=src, dst_ref=dst, send_sem=ss, recv_sem=rs,
            device_id=(ep, core), device_id_type=MESH,
        )

    barrier = pltpu.get_barrier_semaphore()

    def greet(ep, core):
        pl.semaphore_signal(barrier, inc=1, device_id=(ep, core), device_id_type=MESH)

    for peer in (z1 * SIDE + j, pa, pb, pd):
        greet(peer, c)
    greet(me, oc)
    pl.when(mid == 1)(lambda: greet(z3 * SIDE + j, c))

    def cols(k):
        return pl.ds(pl.multiple_of(k * half, 128), half)

    loc = [
        pltpu.make_async_copy(tok.at[:, cols(c)], xd.at[0, 0], sem_l.at[0]),
        pltpu.make_async_copy(ids_h, ids, sem_l.at[1]),
        pltpu.make_async_copy(wg_h.at[0], wg, sem_l.at[2]),
        pltpu.make_async_copy(wu_h.at[0], wu, sem_l.at[3]),
        pltpu.make_async_copy(wd_h.at[0, :, cols(c)], wd.at[c], sem_l.at[4]),
        pltpu.make_async_copy(gates_h, gates, sem_l.at[5]),
    ]
    for cp in loc:
        cp.start()
    pl.semaphore_wait(barrier, 5 + mid)
    loc[0].wait()

    def send_z(nb, k, i, h):
        blk = xd.at[k, i, :, span(h)]
        dst = xd.at[k ^ nb, i, :, span(h)]
        return rdma(blk, dst, s_z.at[nb // 2, k, i, h], r_x.at[k ^ nb, i, h], zs[nb] * SIDE + j, c)

    def send_al(k, h):
        return rdma(
            xd.at[k, 0, :, span(h)], xd.at[k, 1, :, span(h)], s_al.at[k, h], r_x.at[k, 1, h], pa, c
        )

    def landed(k, i, h):
        blk = xd.at[k, i, :, span(h)]
        return rdma(blk, blk, s_al.at[k, h], r_x.at[k, i, h], pa, c)

    groups = (gb, gd, ga)

    def send_b(k, i, h, to=None):
        return rdma(
            sb.at[k, i, :, span(h)], xc.at[c, k, groups[i], :, span(h)],
            s_b.at[k, i, h], r_b.at[k, i, h], pb if to is None else to, c,
        )

    def send_c(k, g):
        blk = xc.at[c, k, g]
        return rdma(blk, blk, s_c.at[k, g], r_c.at[k, g], me, oc)

    def table_z(nb, k, i):
        to = zs[nb] * SIDE + j
        return rdma(wbuf.at[k, i], wbuf.at[k ^ nb, i], s_w.at[nb // 2, k, i], r_w.at[k ^ nb, i], to, c)

    def table_al(k):
        return rdma(wbuf.at[k, 0], wbuf.at[k, 1], s_w.at[2, k, 0], r_w.at[k, 1], pa, c)

    def table_landed(k, i):
        return rdma(wbuf.at[k, i], wbuf.at[k, i], s_w.at[2, k, 0], r_w.at[k, i], pa, c)

    send_d = rdma(wd_h.at[0, :, cols(oc)], wd.at[c], s_d, r_d, me, oc)

    def send_h(k):
        blk = hid.at[k, c]
        return rdma(blk, blk, s_h.at[k], r_h.at[k], me, oc)

    def ret_b(k, i, h, to=None):
        return rdma(
            con.at[k, groups[i], :, span(h)], rb.at[k, i, :, span(h)],
            s_rb.at[k, i, h], r_rb.at[k, i, h], pb if to is None else to, c,
        )

    def ret_a(k, h):
        return rdma(
            dd.at[k, 1, :, span(h)], ra.at[k, :, span(h)], s_ra.at[k, h], r_ra.at[k, h], pa, c
        )

    def ret_z(nb, k, i, h):
        slot = LANDING[nb, k ^ nb]
        return rdma(
            dd.at[k, i, :, span(h)], rz.at[slot, i, :, span(h)],
            s_rz.at[k, i, h], r_rz.at[slot, i, h], zs[nb] * SIDE + j, c,
        )

    def summed(slot, i, h):
        blk = rz.at[slot, i, :, span(h)]
        return rdma(blk, blk, s_rz.at[0, i, h], r_rz.at[slot, i, h], pa, c)

    def tabulate():
        row_of = lax.broadcasted_iota(jnp.int32, (n, rows), 0)
        spread = jnp.zeros((n, rows), F32)
        for t in range(ids.shape[0]):
            spread = spread + jnp.where(ids[t : t + 1] == row_of, gates[t : t + 1], 0.0)
        wbuf[0, 0] = spread

    def place(k, i, experts):
        w = wbuf[k, i]
        routed = jnp.where(w > 0.0, 1.0, 0.0)
        first = lax.broadcasted_iota(jnp.int32, (rows, rows), 0)
        second = lax.broadcasted_iota(jnp.int32, (rows, rows), 1)
        rank = jnp.dot(
            routed.astype(bf), jnp.where(first < second, 1.0, 0.0).astype(bf),
            preferred_element_type=F32,
        )
        rank = jnp.where(w > 0.0, rank, -1.0)
        row_of = lax.broadcasted_iota(jnp.int32, (n, rows), 0)
        slot = lax.broadcasted_iota(jnp.int32, (cap, rows), 0).astype(F32)
        slot_t = lax.broadcasted_iota(jnp.int32, (rows, cap), 1).astype(F32)
        picked = []
        for q, e in enumerate(experts):
            keep = row_of == e
            at = jnp.sum(jnp.where(keep, rank, 0.0), axis=0, keepdims=True)
            gate = jnp.sum(jnp.where(keep, w, 0.0), axis=0, keepdims=True)
            picked.append(jnp.where(slot == at, 1.0, 0.0))
            at_t = jnp.sum(jnp.where(first == second, at, 0.0), axis=1, keepdims=True)
            gate_t = jnp.sum(jnp.where(first == second, gate, 0.0), axis=1, keepdims=True)
            pt[k, i, q] = jnp.where(slot_t == at_t, 1.0, 0.0).astype(bf)
            gc[k, i, q] = jnp.broadcast_to(gate_t, (rows, 128))
        pk[k, i, : len(picked) * cap] = jnp.concatenate(picked, axis=0).astype(bf)

    class Role:
        def __init__(self, name):
            self.name = name
            self.other = {1: MID if name == END else END, 3: MID}
            self.nbs = (1,) if name == END else (1, 3)
            self.seen = set()

        def once(self, key, copy):
            if key not in self.seen:
                self.seen.add(key)
                copy.wait_recv()

        def forwards(self, k, i, h):
            found = []
            for nb in self.nbs:
                to = k ^ nb
                if to == 0 or (self.other[nb] == MID and nb == 1 and k != 0):
                    continue
                if nb == 3 and k not in (0, 1) or nb == 1 and self.name == MID and k == 1:
                    continue
                if i == 0 or FETCH[self.other[nb]][to][h] == "z":
                    found.append(nb)
            return found

        def along(self, k, h):
            return FETCH[self.name][k][h] == "a"

        def beside(self, k, h):
            return GIVE[self.name][k][h] == "a"

        def direct(self, k):
            return FETCH[self.name][k][0] == "d"

        def peers(self, k):
            return (pb, pd, pa) if self.direct(k) else (pb, pb)

        def get(self, k, i, h):
            if (k, i, h) in self.seen:
                return
            self.seen.add((k, i, h))
            if i == 1 and self.direct(k):
                return
            if (k, i) != (0, 0):
                landed(k, i, h).wait_recv()
            for nb in self.forwards(k, i, h):
                send_z(nb, k, i, h).start()
            if i == 0 and self.along(k, h):
                send_al(k, h).start()
            if h == 0:
                if (k, i) == (0, 0):
                    loc[1].wait()
                    loc[5].wait()
                    tabulate()
                else:
                    table_landed(k, i).wait_recv()
                for nb in self.forwards(k, i, 0):
                    table_z(nb, k, i).start()
                if i == 0 and self.along(k, 0):
                    table_al(k).start()

        def compact(self, k, i):
            direct = self.direct(k)
            if direct and i == 1:
                return
            experts = (me, pb, pd, pa) if direct else (me, pb)
            g = 0 if i == 0 else ga
            for h in parts:
                self.get(k, i, h)
                if h == 0:
                    place(k, i, experts)
                at = span(h)
                o = jnp.dot(
                    pk[k, i, : len(experts) * cap], xd[k, i, :, at], preferred_element_type=F32
                )
                xc[c, k, g, :, at] = o[:cap].astype(bf)
                for q, to in enumerate(experts[1:]):
                    sb[k, i + q, :, at] = o[(q + 1) * cap : (q + 2) * cap].astype(bf)
                    send_b(k, i + q, h, to).start()
            send_c(k, g).start()

        def relay(self, k, i):
            if i == 2 and not self.direct(k):
                return
            for h in parts:
                send_b(k, i, h).wait_recv()
            send_c(k, groups[i]).start()

        def up(self, k):
            if "up" not in self.seen:
                self.seen.add("up")
                loc[2].wait()
                loc[3].wait()
            for g in range(4):
                self.once(("c", k, g), send_c(k, g))
            step = min(256, width)

            @pl.loop(0, width // step)
            def _(t):
                at = pl.ds(pl.multiple_of(t * step, step), step)
                x0 = xc[0, k].reshape(SIDE * cap, half)
                x1 = xc[1, k].reshape(SIDE * cap, half)
                g = jnp.dot(x0, wg[:half, at], preferred_element_type=F32)
                g = g + jnp.dot(x1, wg[half:, at], preferred_element_type=F32)
                u = jnp.dot(x0, wu[:half, at], preferred_element_type=F32)
                u = u + jnp.dot(x1, wu[half:, at], preferred_element_type=F32)
                hid[k, c, :, at] = (g / (1.0 + jnp.exp(-g)) * u).astype(bf)

            send_h(k).start()

        def down(self, k):
            if "down" not in self.seen:
                self.seen.add("down")
                loc[4].wait()
                send_d.wait_recv()
            self.once(("h", k), send_h(k))

            for h in parts:
                at = span(h)
                o = jnp.dot(hid[k, 0], wd[0, :, at], preferred_element_type=F32)
                o = o + jnp.dot(hid[k, 1], wd[1, :, at], preferred_element_type=F32)
                con[k, :, :, at] = o.reshape(SIDE, cap, at.size).astype(bf)

        def give(self, k, i):
            if i < len(self.peers(k)):
                for h in parts:
                    ret_b(k, i, h, self.peers(k)[i]).start()

        def incoming(self, k, i, h):
            slots = []
            for nb in self.nbs:
                if (nb, k) in LANDING and not (self.name == END and k != 0):
                    if i == 0 or GIVE[self.other[nb]][k ^ nb][h] == "z":
                        slots.append(LANDING[nb, k])
            return slots

        def toward(self, k):
            return 1 if self.name == END or k == 1 else 3

        def back(self, k, i, h):
            direct = self.direct(k)
            if direct and i == 1:
                return
            g = 0 if i == 0 else ga
            slots = self.incoming(k, i, h)
            others = range(3) if direct else (i,)
            for q in others:
                ret_b(k, q, h).wait_recv()
            for s in slots:
                summed(s, i, h).wait_recv()
            if i == 0 and self.beside(k, h):
                ret_a(k, h).wait_recv()
            at = span(h)
            o = jnp.dot(pt[k, i, 0], con[k, g, :, at], preferred_element_type=F32) * gc[k, i, 0, :, 0:1]
            for q in others:
                e = q - i + 1
                p = jnp.dot(pt[k, i, e], rb[k, q, :, at], preferred_element_type=F32)
                o = o + p * gc[k, i, e, :, 0:1]
            for s in slots:
                o = o + rz[s, i, :, at].astype(F32)
            if i == 0 and self.beside(k, h):
                o = o + ra[k, :, at].astype(F32)
            if (k, i) == (0, 0):
                out[:, at] = o.astype(bf)
                return
            dd[k, i, :, at] = o.astype(bf)
            if i == 1 and self.beside(k, h):
                ret_a(k, h).start()
            else:
                ret_z(self.toward(k), k, i, h).start()

        def finish(self):
            send_d.wait_send()
            for k in range(PLANES):
                for g in range(4):
                    send_c(k, g).wait_send()
                send_h(k).wait_send()
                if self.along(k, 0):
                    table_al(k).wait_send()
                for i in range(2):
                    for nb in self.forwards(k, i, 0):
                        table_z(nb, k, i).wait_send()
                for h in parts:
                    for i in range(len(self.peers(k))):
                        send_b(k, i, h).wait_send()
                        ret_b(k, i, h).wait_send()
                    if self.along(k, h):
                        send_al(k, h).wait_send()
                    if self.beside(k, h):
                        ret_a(k, h).wait_send()
                    for i in range(2):
                        for nb in self.forwards(k, i, h):
                            send_z(nb, k, i, h).wait_send()
                        if k > 0 and (i == 0 or GIVE[self.name][k][h] == "z"):
                            ret_z(self.toward(k), k, i, h).wait_send()

        def run(self, plan):
            for h in parts:
                self.get(0, 0, h)
            self.compact(0, 0)
            send_d.start()
            for what, *at in plan:
                getattr(self, what)(*at)
            self.finish()

    @pl.when(mid == 0)
    def _():
        Role(END).run(PLAN[END])

    @pl.when(mid == 1)
    def _():
        Role(MID).run(PLAN[MID])


PLAN = {
    END: (
        ("compact", 1, 0), ("relay", 0, 0), ("get", 0, 1, 1), ("compact", 0, 1),
        ("relay", 1, 0), ("compact", 1, 1), ("relay", 0, 1), ("compact", 2, 0),
        ("up", 0), ("relay", 1, 1), ("compact", 3, 0), ("up", 1),
        ("compact", 3, 1), ("relay", 3, 0), ("down", 1), ("give", 1, 1),
        ("relay", 3, 1), ("relay", 2, 0), ("compact", 2, 1), ("up", 3),
        ("relay", 2, 1), ("down", 3), ("give", 3, 1), ("give", 3, 0),
        ("up", 2), ("back", 3, 1, 0), ("down", 2), ("give", 2, 1),
        ("get", 0, 1, 0), ("back", 3, 0, 0), ("back", 3, 1, 1), ("back", 2, 1, 0),
        ("down", 0), ("back", 3, 0, 1), ("give", 2, 0), ("give", 1, 0),
        ("back", 1, 1, 1), ("give", 0, 1), ("back", 2, 1, 1), ("back", 1, 1, 0),
        ("back", 2, 0, 0), ("back", 2, 0, 1), ("back", 1, 0, 1), ("back", 0, 1, 0),
        ("back", 0, 1, 1), ("back", 1, 0, 0), ("give", 0, 0), ("back", 0, 0, 0),
        ("back", 0, 0, 1),
    ),
    MID: (
        ("get", 3, 0, 0), ("compact", 1, 0), ("get", 3, 0, 1), ("get", 1, 1, 0),
        ("relay", 1, 0), ("compact", 2, 0), ("compact", 1, 1), ("compact", 2, 1),
        ("get", 2, 0, 0), ("compact", 3, 0), ("compact", 3, 1), ("relay", 1, 1),
        ("get", 3, 1, 0), ("compact", 0, 1), ("relay", 0, 0), ("relay", 2, 1),
        ("relay", 2, 0), ("get", 1, 0, 1), ("get", 3, 1, 1), ("get", 2, 1, 1),
        ("get", 2, 0, 1), ("get", 2, 1, 0), ("up", 1), ("up", 2),
        ("relay", 3, 1), ("down", 1), ("give", 1, 0), ("give", 1, 1),
        ("relay", 0, 1), ("relay", 3, 0), ("down", 2), ("up", 3),
        ("give", 2, 1), ("up", 0), ("give", 2, 0), ("down", 3),
        ("back", 2, 1, 1), ("back", 1, 1, 1), ("give", 3, 1), ("back", 2, 1, 0),
        ("down", 0), ("back", 2, 0, 0), ("give", 3, 0), ("give", 0, 1),
        ("get", 1, 1, 1), ("get", 0, 1, 0), ("back", 2, 0, 1), ("get", 0, 1, 1),
        ("back", 1, 1, 0), ("back", 3, 1, 0), ("get", 1, 0, 0), ("back", 1, 0, 0),
        ("back", 3, 1, 1), ("back", 0, 1, 0), ("back", 0, 1, 1), ("back", 3, 0, 0),
        ("give", 0, 0), ("back", 1, 0, 1), ("back", 3, 0, 1), ("back", 0, 0, 1),
        ("back", 0, 0, 0),
    ),
}


def plane_shards(tokens, expert_ids, routing_gates, w_gate, w_up, w_down):
    n = PLANES * SIDE
    rows, model_width = tokens.shape
    half = model_width // 2
    width = w_gate.shape[2]
    topk = expert_ids.shape[1]
    cap = rows * topk * 9 // (8 * n)
    bf = jnp.bfloat16
    dma = pltpu.SemaphoreType.DMA
    anyspec = pl.BlockSpec(memory_space=pl.ANY)
    return pl.pallas_call(
        kernel,
        out_shape=jax.ShapeDtypeStruct((rows, half), bf),
        in_specs=[anyspec] * 6,
        out_specs=pl.BlockSpec(memory_space=pltpu.VMEM),
        scratch_shapes=[
            pltpu.VMEM((PLANES, 2, rows, half), bf),
            pltpu.VMEM((2, PLANES, SIDE, cap, half), bf),
            pltpu.VMEM((PLANES, 3, cap, half), bf),
            pltpu.VMEM((PLANES, 2, SIDE * cap, rows), bf),
            pltpu.VMEM((PLANES, 2, SIDE, rows, cap), bf),
            pltpu.VMEM((PLANES, 2, SIDE, rows, 128), F32),
            pltpu.VMEM((topk, rows), jnp.int32),
            pltpu.VMEM((topk, rows), F32),
            pltpu.VMEM((PLANES, 2, n, rows), F32),
            pltpu.VMEM((model_width, width), bf),
            pltpu.VMEM((model_width, width), bf),
            pltpu.VMEM((2, width, half), bf),
            pltpu.VMEM((PLANES, 2, SIDE * cap, width), bf),
            pltpu.VMEM((PLANES, SIDE, cap, half), bf),
            pltpu.VMEM((PLANES, 3, cap, half), bf),
            pltpu.VMEM((PLANES, 2, rows, half), bf),
            pltpu.VMEM((PLANES, rows, half), bf),
            pltpu.VMEM((len(LANDING), 2, rows, half), bf),
            dma((6,)),
            dma((2, PLANES, 2, PARTS)), dma((PLANES, PARTS)), dma((PLANES, 2, PARTS)),
            dma((PLANES, 3, PARTS)), dma((PLANES, 3, PARTS)),
            dma((PLANES, SIDE)), dma((PLANES, SIDE)),
            dma((PLANES,)), dma((PLANES,)),
            dma, dma,
            dma((3, PLANES, 2)), dma((PLANES, 2)),
            dma((PLANES, 3, PARTS)), dma((PLANES, 3, PARTS)),
            dma((PLANES, PARTS)), dma((PLANES, PARTS)),
            dma((PLANES, 2, PARTS)), dma((len(LANDING), 2, PARTS)),
        ],
        compiler_params=pltpu.CompilerParams(
            collective_id=0, has_side_effects=True, vmem_limit_bytes=60 << 20
        ),
        cost_estimate=pl.CostEstimate(
            flops=6 * n * cap * model_width * width, bytes_accessed=12 << 20,
            transcendentals=n * cap * width,
        ),
        name="planes",
    )(tokens, expert_ids.T, routing_gates.T, w_gate, w_up, w_down)


def solution(mesh):
    small = mesh.shape["ep"] == PLANES * SIDE and mesh.shape["etp"] == 2
    return jax.shard_map(
        plane_shards if small else plain_shards,
        mesh=mesh,
        in_specs=(
            P("ep", None),
            P("ep", None),
            P("ep", None),
            P("ep", None, "etp"),
            P("ep", None, "etp"),
            P("ep", "etp", None),
        ),
        out_specs=P("ep", "etp"),
        check_vma=False,
    )
```

```python
import functools

import jax
import jax.numpy as jnp
from jax import lax
from jax.experimental import pallas as pl
from jax.experimental.pallas import tpu as pltpu
from jax.sharding import PartitionSpec as P

MESH = pl.DeviceIdType.MESH
F32 = jnp.float32
PLANES = 4
SIDE = 4
PARTS = 3
END, MID = 0, 1
GET, COMPACT, RELAY, UP, DOWN, GIVE_BACK, BACK = range(7)
FETCH = {
    END: {0: "aaa", 1: "zzz", 2: "aaa", 3: "aaa"},
    MID: {0: "aaa", 1: "zzz", 2: "aaa", 3: "aaa"},
}
GIVE = {
    END: {0: "aaa", 1: "aaa", 2: "zzz", 3: "aaa"},
    MID: {0: "aaa", 1: "aaa", 2: "zzz", 3: "aaa"},
}
LANDING = {(1, 0): 0, (1, 2): 1, (1, 3): 2, (3, 0): 3, (3, 1): 4}


def plain_shards(tokens, expert_ids, routing_gates, w_gate, w_up, w_down):
    ep_count = lax.axis_size("ep")
    tok_rows, topk_count = expert_ids.shape
    model_width = tokens.shape[1]
    half_width = model_width // lax.axis_size("etp")
    capacity = max(2, tok_rows * topk_count * 9 // (8 * ep_count))
    flat_ids = expert_ids.reshape(-1)
    onehot = (flat_ids[:, None] == jnp.arange(ep_count, dtype=jnp.int32)[None, :]).astype(jnp.bfloat16)
    row_range = jnp.arange(tok_rows * topk_count, dtype=jnp.int32)
    earlier = (row_range[None, :] < row_range[:, None]).astype(jnp.bfloat16)
    counted = jnp.dot(earlier, onehot, preferred_element_type=F32)
    row_ranks = jnp.sum(counted * onehot.astype(F32), axis=1).astype(jnp.int32)
    slot_index = flat_ids * capacity + row_ranks
    slot_table = slot_index.reshape(tok_rows, topk_count)
    slot_range = jnp.arange(ep_count * capacity, dtype=jnp.int32)
    dispatch = jnp.any(slot_range[:, None, None] == slot_table[None, :, :], axis=2).astype(
        jnp.bfloat16
    )
    outgoing = jnp.dot(dispatch, tokens, preferred_element_type=jnp.float32).astype(jnp.bfloat16)
    outgoing = outgoing.reshape(ep_count, capacity, model_width)
    arrived = lax.all_to_all(outgoing, "ep", split_axis=0, concat_axis=0, tiled=True)
    expert_rows = arrived.reshape(ep_count * capacity, model_width)
    gate_val = jnp.dot(expert_rows, w_gate[0], preferred_element_type=jnp.float32)
    up_val = jnp.dot(expert_rows, w_up[0], preferred_element_type=jnp.float32)
    hidden = (jax.nn.silu(gate_val) * up_val).astype(jnp.bfloat16)
    partial_value = jnp.dot(hidden, w_down[0], preferred_element_type=jnp.float32)
    summed = lax.psum_scatter(
        partial_value.astype(jnp.bfloat16), "etp", scatter_dimension=1, tiled=True
    )
    outgoing_back = summed.reshape(ep_count, capacity, half_width)
    returned = lax.all_to_all(outgoing_back, "ep", split_axis=0, concat_axis=0, tiled=True).reshape(
        -1, half_width
    )
    picked = returned[slot_index].reshape(tok_rows, topk_count, half_width).astype(jnp.float32)
    combined = jnp.einsum("tk,tkd->td", routing_gates, picked)
    return combined.astype(jnp.bfloat16)


def kernel(
    tok, ids_h, gates_h, wg_h, wu_h, wd_h, out,
    xd, xc, sb, pk, pt, gc, ids, gates, wbuf, wg, wu, wd, hid, con, rb, dd, ra, rz,
    sem_l, s_z, s_al, r_x, s_b, r_b, s_c, r_c, s_h, r_h, s_d, r_d, s_w, r_w,
    s_rb, r_rb, s_ra, r_ra, s_rz, r_rz,
):
    me, c = lax.axis_index("ep"), lax.axis_index("etp")
    n = PLANES * SIDE
    oc = 1 - c
    x, y, z = me % 2, (me // 2) % 2, me // 4
    j = me % 4
    xj, yj = j + 1 - 2 * x, j + 2 - 4 * y
    ja = xj + c * (yj - xj)
    jb = yj + c * (xj - yj)
    pa, pb, pd = me - j + ja, me - j + jb, me - j + xj + yj - j
    ga, gb, gd = 1 + c, 2 - c, 3
    z1, z2, z3 = z + 1 - 2 * (z % 2), z + 2 - 4 * (z // 2), 3 - z
    zs = [z, z1, z2, z3]
    mid = (z % 2 + z // 2) % 2
    rows, half = out.shape
    width = wg.shape[1]
    cap = sb.shape[2]
    bf = jnp.bfloat16
    tile = 256
    tiles = half // tile
    cuts = [(p * tiles + PARTS - 1) // PARTS for p in range(PARTS + 1)]
    parts = range(PARTS)

    def span(h):
        return pl.ds(cuts[h] * tile, (cuts[h + 1] - cuts[h]) * tile)

    def rdma(src, dst, ss, rs, ep, core):
        return pltpu.make_async_remote_copy(
            src_ref=src, dst_ref=dst, send_sem=ss, recv_sem=rs,
            device_id=(ep, core), device_id_type=MESH,
        )

    barrier = pltpu.get_barrier_semaphore()

    def greet(ep, core):
        pl.semaphore_signal(barrier, inc=1, device_id=(ep, core), device_id_type=MESH)

    for peer in (z1 * SIDE + j, pa, pb, pd):
        greet(peer, c)
    greet(me, oc)
    pl.when(mid == 1)(lambda: greet(z3 * SIDE + j, c))

    def cols(k):
        return pl.ds(pl.multiple_of(k * half, 128), half)

    loc = [
        pltpu.make_async_copy(tok.at[:, cols(c)], xd.at[0, 0], sem_l.at[0]),
        pltpu.make_async_copy(ids_h, ids, sem_l.at[1]),
        pltpu.make_async_copy(wg_h.at[0], wg, sem_l.at[2]),
        pltpu.make_async_copy(wu_h.at[0], wu, sem_l.at[3]),
        pltpu.make_async_copy(wd_h.at[0, :, cols(c)], wd.at[c], sem_l.at[4]),
        pltpu.make_async_copy(gates_h, gates, sem_l.at[5]),
    ]
    for cp in loc:
        cp.start()
    pl.semaphore_wait(barrier, 5 + mid)
    loc[0].wait()

    def send_z(nb, k, i, h):
        blk = xd.at[k, i, :, span(h)]
        dst = xd.at[k ^ nb, i, :, span(h)]
        return rdma(blk, dst, s_z.at[nb // 2, k, i, h], r_x.at[k ^ nb, i, h], zs[nb] * SIDE + j, c)

    def send_al(k, h):
        return rdma(
            xd.at[k, 0, :, span(h)], xd.at[k, 1, :, span(h)], s_al.at[k, h], r_x.at[k, 1, h], pa, c
        )

    def landed(k, i, h):
        blk = xd.at[k, i, :, span(h)]
        return rdma(blk, blk, s_al.at[k, h], r_x.at[k, i, h], pa, c)

    groups = (gb, gd, ga)

    def send_b(k, i, h, to=None):
        return rdma(
            sb.at[k, i, :, span(h)], xc.at[c, k, groups[i], :, span(h)],
            s_b.at[k, i, h], r_b.at[k, i, h], pb if to is None else to, c,
        )

    def send_c(k, g):
        blk = xc.at[c, k, g]
        return rdma(blk, blk, s_c.at[k, g], r_c.at[k, g], me, oc)

    def table_z(nb, k, i):
        to = zs[nb] * SIDE + j
        return rdma(wbuf.at[k, i], wbuf.at[k ^ nb, i], s_w.at[nb // 2, k, i], r_w.at[k ^ nb, i], to, c)

    def table_al(k):
        return rdma(wbuf.at[k, 0], wbuf.at[k, 1], s_w.at[2, k, 0], r_w.at[k, 1], pa, c)

    def table_landed(k, i):
        return rdma(wbuf.at[k, i], wbuf.at[k, i], s_w.at[2, k, 0], r_w.at[k, i], pa, c)

    send_d = rdma(wd_h.at[0, :, cols(oc)], wd.at[c], s_d, r_d, me, oc)

    def send_h(k):
        blk = hid.at[k, c]
        return rdma(blk, blk, s_h.at[k], r_h.at[k], me, oc)

    def ret_b(k, i, h, to=None):
        return rdma(
            con.at[k, groups[i], :, span(h)], rb.at[k, i, :, span(h)],
            s_rb.at[k, i, h], r_rb.at[k, i, h], pb if to is None else to, c,
        )

    def ret_a(k, h):
        return rdma(
            dd.at[k, 1, :, span(h)], ra.at[k, :, span(h)], s_ra.at[k, h], r_ra.at[k, h], pa, c
        )

    def ret_z(nb, k, i, h):
        slot = LANDING[nb, k ^ nb]
        return rdma(
            dd.at[k, i, :, span(h)], rz.at[slot, i, :, span(h)],
            s_rz.at[k, i, h], r_rz.at[slot, i, h], zs[nb] * SIDE + j, c,
        )

    def summed(slot, i, h):
        blk = rz.at[slot, i, :, span(h)]
        return rdma(blk, blk, s_rz.at[0, i, h], r_rz.at[slot, i, h], pa, c)

    def tabulate():
        row_of = lax.broadcasted_iota(jnp.int32, (n, rows), 0)
        spread = jnp.zeros((n, rows), F32)
        for t in range(ids.shape[0]):
            spread = spread + jnp.where(ids[t : t + 1] == row_of, gates[t : t + 1], 0.0)
        wbuf[0, 0] = spread

    def place(k, i, experts):
        w = wbuf[k, i]
        routed = jnp.where(w > 0.0, 1.0, 0.0)
        first = lax.broadcasted_iota(jnp.int32, (rows, rows), 0)
        second = lax.broadcasted_iota(jnp.int32, (rows, rows), 1)
        rank = jnp.dot(
            routed.astype(bf), jnp.where(first < second, 1.0, 0.0).astype(bf),
            preferred_element_type=F32,
        )
        rank = jnp.where(w > 0.0, rank, -1.0)
        row_of = lax.broadcasted_iota(jnp.int32, (n, rows), 0)
        slot = lax.broadcasted_iota(jnp.int32, (cap, rows), 0).astype(F32)
        slot_t = lax.broadcasted_iota(jnp.int32, (rows, cap), 1).astype(F32)
        picked = []
        for q, e in enumerate(experts):
            keep = row_of == e
            at = jnp.sum(jnp.where(keep, rank, 0.0), axis=0, keepdims=True)
            gate = jnp.sum(jnp.where(keep, w, 0.0), axis=0, keepdims=True)
            picked.append(jnp.where(slot == at, 1.0, 0.0))
            at_t = jnp.sum(jnp.where(first == second, at, 0.0), axis=1, keepdims=True)
            gate_t = jnp.sum(jnp.where(first == second, gate, 0.0), axis=1, keepdims=True)
            pt[k, i, q] = jnp.where(slot_t == at_t, 1.0, 0.0).astype(bf)
            gc[k, i, q] = jnp.broadcast_to(gate_t, (rows, 128))
        pk[k, i, : len(picked) * cap] = jnp.concatenate(picked, axis=0).astype(bf)

    class Role:
        def __init__(self, name):
            self.name = name
            self.other = {1: MID if name == END else END, 3: MID}
            self.nbs = (1,) if name == END else (1, 3)
            self.seen = set()

        def once(self, key, copy):
            if key not in self.seen:
                self.seen.add(key)
                copy.wait_recv()

        def forwards(self, k, i, h):
            found = []
            for nb in self.nbs:
                to = k ^ nb
                if to == 0 or (self.other[nb] == MID and nb == 1 and k != 0):
                    continue
                if nb == 3 and k not in (0, 1) or nb == 1 and self.name == MID and k == 1:
                    continue
                if i == 0 or FETCH[self.other[nb]][to][h] == "z":
                    found.append(nb)
            return found

        def along(self, k, h):
            return FETCH[self.name][k][h] == "a"

        def beside(self, k, h):
            return GIVE[self.name][k][h] == "a"

        def direct(self, k):
            return FETCH[self.name][k][0] == "d"

        def peers(self, k):
            return (pb, pd, pa) if self.direct(k) else (pb, pb)

        def get(self, k, i, h):
            if (k, i, h) in self.seen:
                return
            self.seen.add((k, i, h))
            if (k, i) != (0, 0):
                landed(k, i, h).wait_recv()
            for nb in self.forwards(k, i, h):
                send_z(nb, k, i, h).start()
            if i == 0 and self.along(k, h):
                send_al(k, h).start()
            if h == 0:
                if (k, i) == (0, 0):
                    loc[1].wait()
                    loc[5].wait()
                    tabulate()
                else:
                    table_landed(k, i).wait_recv()
                for nb in self.forwards(k, i, 0):
                    table_z(nb, k, i).start()
                if i == 0 and self.along(k, 0):
                    table_al(k).start()

        def compact(self, k, i, h):
            experts = (me, pb, pd, pa) if self.direct(k) else (me, pb)
            g = 0 if i == 0 else ga
            self.get(k, i, h)
            if ("place", k, i) not in self.seen:
                self.seen.add(("place", k, i))
                self.get(k, i, 0)
                place(k, i, experts)
            at = span(h)
            o = jnp.dot(pk[k, i, : len(experts) * cap], xd[k, i, :, at], preferred_element_type=F32)
            xc[c, k, g, :, at] = o[:cap].astype(bf)
            for q, to in enumerate(experts[1:]):
                sb[k, i + q, :, at] = o[(q + 1) * cap : (q + 2) * cap].astype(bf)
                send_b(k, i + q, h, to).start()
            self.seen.add(("cut", k, i, h))
            if all(("cut", k, i, p) in self.seen for p in parts):
                send_c(k, g).start()

        def relay(self, k, i):
            for h in parts:
                send_b(k, i, h).wait_recv()
            send_c(k, groups[i]).start()

        def up(self, k):
            if "up" not in self.seen:
                self.seen.add("up")
                loc[2].wait()
                loc[3].wait()
            for g in range(4):
                self.once(("c", k, g), send_c(k, g))
            step = min(256, width)

            @pl.loop(0, width // step)
            def _(t):
                at = pl.ds(pl.multiple_of(t * step, step), step)
                x0 = xc[0, k].reshape(SIDE * cap, half)
                x1 = xc[1, k].reshape(SIDE * cap, half)
                g = jnp.dot(x0, wg[:half, at], preferred_element_type=F32)
                g = g + jnp.dot(x1, wg[half:, at], preferred_element_type=F32)
                u = jnp.dot(x0, wu[:half, at], preferred_element_type=F32)
                u = u + jnp.dot(x1, wu[half:, at], preferred_element_type=F32)
                hid[k, c, :, at] = (g / (1.0 + jnp.exp(-g)) * u).astype(bf)

            send_h(k).start()

        def down(self, k, h):
            if "down" not in self.seen:
                self.seen.add("down")
                loc[4].wait()
                send_d.wait_recv()
            if ("h", k) not in self.seen:
                self.once(("h", k), send_h(k))
            at = span(h)

            o = jnp.dot(hid[k, 0], wd[0, :, at], preferred_element_type=F32)
            o = o + jnp.dot(hid[k, 1], wd[1, :, at], preferred_element_type=F32)
            con[k, :, :, at] = o.reshape(SIDE, cap, at.size).astype(bf)

        def give(self, k, i, h):
            ret_b(k, i, h, self.peers(k)[i]).start()

        def incoming(self, k, i, h):
            slots = []
            for nb in self.nbs:
                if (nb, k) in LANDING and not (self.name == END and k != 0):
                    if i == 0 or GIVE[self.other[nb]][k ^ nb][h] == "z":
                        slots.append(LANDING[nb, k])
            return slots

        def toward(self, k):
            return 1 if self.name == END or k == 1 else 3

        def back(self, k, i, h):
            direct = self.direct(k)
            g = 0 if i == 0 else ga
            slots = self.incoming(k, i, h)
            others = range(3) if direct else (i,)
            for q in others:
                ret_b(k, q, h).wait_recv()
            for s in slots:
                summed(s, i, h).wait_recv()
            if i == 0 and self.beside(k, h):
                ret_a(k, h).wait_recv()
            at = span(h)
            o = jnp.dot(pt[k, i, 0], con[k, g, :, at], preferred_element_type=F32) * gc[k, i, 0, :, 0:1]
            for q in others:
                e = q - i + 1
                p = jnp.dot(pt[k, i, e], rb[k, q, :, at], preferred_element_type=F32)
                o = o + p * gc[k, i, e, :, 0:1]
            for s in slots:
                o = o + rz[s, i, :, at].astype(F32)
            if i == 0 and self.beside(k, h):
                o = o + ra[k, :, at].astype(F32)
            if (k, i) == (0, 0):
                out[:, at] = o.astype(bf)
                return
            dd[k, i, :, at] = o.astype(bf)
            if i == 1 and self.beside(k, h):
                ret_a(k, h).start()
            else:
                ret_z(self.toward(k), k, i, h).start()

        def finish(self):
            send_d.wait_send()
            for k in range(PLANES):
                for g in range(4):
                    send_c(k, g).wait_send()
                send_h(k).wait_send()
                if self.along(k, 0):
                    table_al(k).wait_send()
                for i in range(2):
                    for nb in self.forwards(k, i, 0):
                        table_z(nb, k, i).wait_send()
                for h in parts:
                    for i in range(len(self.peers(k))):
                        send_b(k, i, h).wait_send()
                        ret_b(k, i, h).wait_send()
                    if self.along(k, h):
                        send_al(k, h).wait_send()
                    if self.beside(k, h):
                        ret_a(k, h).wait_send()
                    for i in range(2):
                        for nb in self.forwards(k, i, h):
                            send_z(nb, k, i, h).wait_send()
                        if k > 0 and (i == 0 or GIVE[self.name][k][h] == "z"):
                            ret_z(self.toward(k), k, i, h).wait_send()

        def run(self, plan):
            for h in parts:
                self.get(0, 0, h)
            send_d.start()
            steps = (self.get, self.compact, self.relay, self.up, self.down, self.give, self.back)
            for what, *at in plan:
                steps[what](*at)
            self.finish()

    @pl.when(mid == 0)
    def _():
        Role(END).run(PLAN[END])

    @pl.when(mid == 1)
    def _():
        Role(MID).run(PLAN[MID])


PLAN = {
    END: (
        (COMPACT, 0, 0, 0), (COMPACT, 0, 0, 1), (COMPACT, 0, 1, 0), (COMPACT, 0, 1, 1),
        (COMPACT, 0, 1, 2), (COMPACT, 0, 0, 2), (COMPACT, 1, 0, 1), (RELAY, 0, 0),
        (RELAY, 0, 1), (COMPACT, 1, 0, 2), (COMPACT, 1, 0, 0), (COMPACT, 2, 0, 0),
        (COMPACT, 2, 0, 2), (UP, 0), (COMPACT, 2, 0, 1), (COMPACT, 2, 1, 2),
        (COMPACT, 2, 1, 0), (DOWN, 0, 1), (COMPACT, 2, 1, 1), (RELAY, 2, 0),
        (DOWN, 0, 2), (COMPACT, 3, 0, 0), (DOWN, 0, 0), (RELAY, 2, 1),
        (COMPACT, 3, 0, 1), (COMPACT, 3, 0, 2), (UP, 2), (COMPACT, 3, 1, 0),
        (COMPACT, 3, 1, 1), (COMPACT, 3, 1, 2), (DOWN, 2, 2), (GIVE_BACK, 2, 1, 2),
        (DOWN, 2, 1), (GIVE_BACK, 2, 1, 1), (GIVE_BACK, 0, 1, 0), (RELAY, 3, 0),
        (COMPACT, 1, 1, 0), (GIVE_BACK, 2, 0, 2), (COMPACT, 1, 1, 1), (RELAY, 3, 1),
        (BACK, 2, 1, 2), (DOWN, 2, 0), (BACK, 2, 1, 1), (GIVE_BACK, 2, 0, 0),
        (GIVE_BACK, 0, 1, 2), (GIVE_BACK, 2, 1, 0), (UP, 3), (BACK, 2, 0, 2),
        (COMPACT, 1, 1, 2), (GIVE_BACK, 2, 0, 1), (DOWN, 3, 1), (GIVE_BACK, 3, 0, 1),
        (DOWN, 3, 2), (RELAY, 1, 0), (GIVE_BACK, 3, 1, 2), (GIVE_BACK, 3, 1, 1),
        (BACK, 2, 1, 0), (DOWN, 3, 0), (GIVE_BACK, 3, 1, 0), (RELAY, 1, 1),
        (BACK, 2, 0, 1), (GIVE_BACK, 3, 0, 2), (BACK, 3, 1, 2), (BACK, 3, 1, 1),
        (UP, 1), (GIVE_BACK, 3, 0, 0), (BACK, 3, 1, 0), (BACK, 3, 0, 2),
        (BACK, 3, 0, 1), (DOWN, 1, 1), (GIVE_BACK, 1, 0, 1), (DOWN, 1, 0),
        (DOWN, 1, 2), (GIVE_BACK, 1, 1, 2), (GIVE_BACK, 1, 0, 0), (BACK, 3, 0, 0),
        (GIVE_BACK, 1, 1, 0), (GIVE_BACK, 0, 0, 2), (GIVE_BACK, 1, 1, 1), (GIVE_BACK, 1, 0, 2),
        (BACK, 2, 0, 0), (GIVE_BACK, 0, 1, 1), (BACK, 1, 1, 2), (BACK, 1, 1, 1),
        (BACK, 1, 1, 0), (BACK, 1, 0, 2), (BACK, 0, 1, 1), (GIVE_BACK, 0, 0, 1),
        (BACK, 1, 0, 1), (BACK, 0, 1, 0), (BACK, 1, 0, 0), (GIVE_BACK, 0, 0, 0),
        (BACK, 0, 0, 1), (BACK, 0, 1, 2), (BACK, 0, 0, 2), (BACK, 0, 0, 0),
    ),
    MID: (
        (COMPACT, 0, 0, 0), (COMPACT, 3, 0, 0), (COMPACT, 1, 0, 1), (COMPACT, 3, 0, 2),
        (COMPACT, 3, 0, 1), (COMPACT, 3, 1, 0), (COMPACT, 3, 1, 2), (COMPACT, 1, 0, 0),
        (COMPACT, 2, 0, 0), (COMPACT, 3, 1, 1), (COMPACT, 0, 0, 1), (COMPACT, 2, 0, 1),
        (RELAY, 3, 0), (COMPACT, 1, 0, 2), (COMPACT, 0, 0, 2), (COMPACT, 2, 0, 2),
        (GET, 0, 1, 0), (RELAY, 3, 1), (COMPACT, 1, 1, 0), (COMPACT, 2, 1, 1),
        (COMPACT, 1, 1, 2), (RELAY, 1, 0), (COMPACT, 2, 1, 2), (COMPACT, 2, 1, 0),
        (UP, 3), (COMPACT, 1, 1, 1), (COMPACT, 0, 1, 1), (RELAY, 0, 0),
        (DOWN, 3, 1), (COMPACT, 0, 1, 2), (RELAY, 2, 0), (RELAY, 2, 1),
        (DOWN, 3, 0), (DOWN, 3, 2), (GIVE_BACK, 3, 0, 1), (RELAY, 1, 1),
        (GIVE_BACK, 3, 1, 1), (COMPACT, 0, 1, 0), (UP, 2), (GIVE_BACK, 3, 0, 0),
        (GIVE_BACK, 3, 1, 2), (UP, 1), (GIVE_BACK, 3, 0, 2), (DOWN, 2, 2),
        (GIVE_BACK, 2, 1, 2), (DOWN, 2, 0), (GIVE_BACK, 2, 1, 0), (GIVE_BACK, 3, 1, 0),
        (DOWN, 1, 0), (DOWN, 2, 1), (GIVE_BACK, 2, 1, 1), (GIVE_BACK, 2, 0, 1),
        (GIVE_BACK, 1, 1, 0), (RELAY, 0, 1), (DOWN, 1, 2), (GIVE_BACK, 1, 1, 2),
        (BACK, 2, 1, 2), (BACK, 3, 1, 2), (BACK, 2, 1, 0), (UP, 0),
        (GIVE_BACK, 1, 0, 0), (GIVE_BACK, 1, 0, 2), (BACK, 3, 1, 1), (DOWN, 1, 1),
        (DOWN, 0, 2), (DOWN, 0, 1), (GIVE_BACK, 2, 0, 0), (GIVE_BACK, 0, 1, 1),
        (GIVE_BACK, 2, 0, 2), (GIVE_BACK, 1, 1, 1), (BACK, 2, 1, 1), (GIVE_BACK, 0, 0, 1),
        (GIVE_BACK, 1, 0, 1), (BACK, 3, 0, 1), (BACK, 1, 1, 2), (DOWN, 0, 0),
        (BACK, 2, 0, 2), (BACK, 3, 1, 0), (BACK, 1, 1, 1), (GIVE_BACK, 0, 1, 0),
        (BACK, 2, 0, 1), (GIVE_BACK, 0, 1, 2), (GIVE_BACK, 0, 0, 0), (BACK, 2, 0, 0),
        (BACK, 1, 0, 2), (BACK, 3, 0, 2), (BACK, 1, 1, 0), (BACK, 0, 1, 0),
        (BACK, 1, 0, 1), (BACK, 3, 0, 0), (BACK, 0, 1, 1), (BACK, 0, 1, 2),
        (BACK, 1, 0, 0), (GIVE_BACK, 0, 0, 2), (BACK, 0, 0, 2), (BACK, 0, 0, 1),
        (BACK, 0, 0, 0),
    ),
}


def plane_shards(tokens, expert_ids, routing_gates, w_gate, w_up, w_down):
    n = PLANES * SIDE
    rows, model_width = tokens.shape
    half = model_width // 2
    width = w_gate.shape[2]
    topk = expert_ids.shape[1]
    cap = rows * topk * 9 // (8 * n)
    bf = jnp.bfloat16
    dma = pltpu.SemaphoreType.DMA
    anyspec = pl.BlockSpec(memory_space=pl.ANY)
    return pl.pallas_call(
        kernel,
        out_shape=pltpu.VMEM((rows, half), bf),
        in_specs=[anyspec] * 6,
        out_specs=pl.BlockSpec(memory_space=pltpu.VMEM),
        scratch_shapes=[
            pltpu.VMEM((PLANES, 2, rows, half), bf),
            pltpu.VMEM((2, PLANES, SIDE, cap, half), bf),
            pltpu.VMEM((PLANES, 3, cap, half), bf),
            pltpu.VMEM((PLANES, 2, SIDE * cap, rows), bf),
            pltpu.VMEM((PLANES, 2, SIDE, rows, cap), bf),
            pltpu.VMEM((PLANES, 2, SIDE, rows, 128), F32),
            pltpu.VMEM((topk, rows), jnp.int32),
            pltpu.VMEM((topk, rows), F32),
            pltpu.VMEM((PLANES, 2, n, rows), F32),
            pltpu.VMEM((model_width, width), bf),
            pltpu.VMEM((model_width, width), bf),
            pltpu.VMEM((2, width, half), bf),
            pltpu.VMEM((PLANES, 2, SIDE * cap, width), bf),
            pltpu.VMEM((PLANES, SIDE, cap, half), bf),
            pltpu.VMEM((PLANES, 3, cap, half), bf),
            pltpu.VMEM((PLANES, 2, rows, half), bf),
            pltpu.VMEM((PLANES, rows, half), bf),
            pltpu.VMEM((len(LANDING), 2, rows, half), bf),
            dma((6,)),
            dma((2, PLANES, 2, PARTS)), dma((PLANES, PARTS)), dma((PLANES, 2, PARTS)),
            dma((PLANES, 3, PARTS)), dma((PLANES, 3, PARTS)),
            dma((PLANES, SIDE)), dma((PLANES, SIDE)),
            dma((PLANES,)), dma((PLANES,)),
            dma, dma,
            dma((3, PLANES, 2)), dma((PLANES, 2)),
            dma((PLANES, 3, PARTS)), dma((PLANES, 3, PARTS)),
            dma((PLANES, PARTS)), dma((PLANES, PARTS)),
            dma((PLANES, 2, PARTS)), dma((len(LANDING), 2, PARTS)),
        ],
        compiler_params=pltpu.CompilerParams(
            collective_id=0, has_side_effects=True, vmem_limit_bytes=60 << 20
        ),
        cost_estimate=pl.CostEstimate(
            flops=6 * n * cap * model_width * width, bytes_accessed=12 << 20,
            transcendentals=n * cap * width,
        ),
        name="planes",
    )(tokens, expert_ids.T, routing_gates.T, w_gate, w_up, w_down)


def solution(mesh):
    small = mesh.shape["ep"] == PLANES * SIDE and mesh.shape["etp"] == 2
    return jax.shard_map(
        plane_shards if small else plain_shards,
        mesh=mesh,
        in_specs=(
            P("ep", None),
            P("ep", None),
            P("ep", None),
            P("ep", None, "etp"),
            P("ep", None, "etp"),
            P("ep", "etp", None),
        ),
        out_specs=P("ep", "etp"),
        check_vma=False,
    )
```

```python
import functools

import jax
import jax.numpy as jnp
from jax import lax
from jax.experimental import pallas as pl
from jax.experimental.pallas import tpu as pltpu
from jax.sharding import PartitionSpec as P

MESH = pl.DeviceIdType.MESH
F32 = jnp.float32
PLANES = 4
SIDE = 4
PARTS = 3
END, MID = 0, 1
GET, COMPACT, RELAY, UP, DOWN, GIVE_BACK, BACK = range(7)
FETCH = {
    END: {0: "aaa", 1: "aaa", 2: "aaz", 3: "aza"},
    MID: {0: "aaa", 1: "aaa", 2: "azz", 3: "zaa"},
}
GIVE = {
    END: {0: "aaa", 1: "azz", 2: "aaa", 3: "aza"},
    MID: {0: "aaa", 1: "zzz", 2: "zza", 3: "aaa"},
}
LANDING = {(1, 0): 0, (1, 2): 1, (1, 3): 2, (3, 0): 3, (3, 1): 4}


def plain_shards(tokens, expert_ids, routing_gates, w_gate, w_up, w_down):
    ep_count = lax.axis_size("ep")
    tok_rows, topk_count = expert_ids.shape
    model_width = tokens.shape[1]
    half_width = model_width // lax.axis_size("etp")
    capacity = max(2, tok_rows * topk_count * 9 // (8 * ep_count))
    flat_ids = expert_ids.reshape(-1)
    onehot = (flat_ids[:, None] == jnp.arange(ep_count, dtype=jnp.int32)[None, :]).astype(jnp.bfloat16)
    row_range = jnp.arange(tok_rows * topk_count, dtype=jnp.int32)
    earlier = (row_range[None, :] < row_range[:, None]).astype(jnp.bfloat16)
    counted = jnp.dot(earlier, onehot, preferred_element_type=F32)
    row_ranks = jnp.sum(counted * onehot.astype(F32), axis=1).astype(jnp.int32)
    slot_index = flat_ids * capacity + row_ranks
    slot_table = slot_index.reshape(tok_rows, topk_count)
    slot_range = jnp.arange(ep_count * capacity, dtype=jnp.int32)
    dispatch = jnp.any(slot_range[:, None, None] == slot_table[None, :, :], axis=2).astype(
        jnp.bfloat16
    )
    outgoing = jnp.dot(dispatch, tokens, preferred_element_type=jnp.float32).astype(jnp.bfloat16)
    outgoing = outgoing.reshape(ep_count, capacity, model_width)
    arrived = lax.all_to_all(outgoing, "ep", split_axis=0, concat_axis=0, tiled=True)
    expert_rows = arrived.reshape(ep_count * capacity, model_width)
    gate_val = jnp.dot(expert_rows, w_gate[0], preferred_element_type=jnp.float32)
    up_val = jnp.dot(expert_rows, w_up[0], preferred_element_type=jnp.float32)
    hidden = (jax.nn.silu(gate_val) * up_val).astype(jnp.bfloat16)
    partial_value = jnp.dot(hidden, w_down[0], preferred_element_type=jnp.float32)
    summed = lax.psum_scatter(
        partial_value.astype(jnp.bfloat16), "etp", scatter_dimension=1, tiled=True
    )
    outgoing_back = summed.reshape(ep_count, capacity, half_width)
    returned = lax.all_to_all(outgoing_back, "ep", split_axis=0, concat_axis=0, tiled=True).reshape(
        -1, half_width
    )
    picked = returned[slot_index].reshape(tok_rows, topk_count, half_width).astype(jnp.float32)
    combined = jnp.einsum("tk,tkd->td", routing_gates, picked)
    return combined.astype(jnp.bfloat16)


def kernel(
    tok, ids_h, gates_h, wg_h, wu_h, wd_h, out,
    xd, xc, sb, pk, pt, gc, ids, gates, wbuf, wg, wu, wd, hid, con, rb, dd, ra, rz,
    sem_l, s_z, s_al, r_x, s_b, r_b, s_c, r_c, s_h, r_h, s_d, r_d, s_w, r_w,
    s_rb, r_rb, s_ra, r_ra, s_rz, r_rz,
):
    me, c = lax.axis_index("ep"), lax.axis_index("etp")
    n = PLANES * SIDE
    oc = 1 - c
    x, y, z = me % 2, (me // 2) % 2, me // 4
    j = me % 4
    xj, yj = j + 1 - 2 * x, j + 2 - 4 * y
    ja = xj + c * (yj - xj)
    jb = yj + c * (xj - yj)
    pa, pb, pd = me - j + ja, me - j + jb, me - j + xj + yj - j
    ga, gb, gd = 1 + c, 2 - c, 3
    z1, z2, z3 = z + 1 - 2 * (z % 2), z + 2 - 4 * (z // 2), 3 - z
    zs = [z, z1, z2, z3]
    mid = (z % 2 + z // 2) % 2
    rows, half = out.shape
    width = wg.shape[1]
    cap = sb.shape[2]
    bf = jnp.bfloat16
    tile = 256
    tiles = half // tile
    cuts = [(p * tiles + PARTS - 1) // PARTS for p in range(PARTS + 1)]
    parts = range(PARTS)

    def span(h):
        return pl.ds(cuts[h] * tile, (cuts[h + 1] - cuts[h]) * tile)

    def rdma(src, dst, ss, rs, ep, core):
        return pltpu.make_async_remote_copy(
            src_ref=src, dst_ref=dst, send_sem=ss, recv_sem=rs,
            device_id=(ep, core), device_id_type=MESH,
        )

    barrier = pltpu.get_barrier_semaphore()

    def greet(ep, core):
        pl.semaphore_signal(barrier, inc=1, device_id=(ep, core), device_id_type=MESH)

    for peer in (z1 * SIDE + j, pa, pb, pd):
        greet(peer, c)
    greet(me, oc)
    pl.when(mid == 1)(lambda: greet(z3 * SIDE + j, c))

    def cols(k):
        return pl.ds(pl.multiple_of(k * half, 128), half)

    loc = [
        pltpu.make_async_copy(tok.at[:, cols(c)], xd.at[0, 0], sem_l.at[0]),
        pltpu.make_async_copy(ids_h, ids, sem_l.at[1]),
        pltpu.make_async_copy(wg_h.at[0], wg, sem_l.at[2]),
        pltpu.make_async_copy(wu_h.at[0], wu, sem_l.at[3]),
        pltpu.make_async_copy(wd_h.at[0, :, cols(c)], wd.at[c], sem_l.at[4]),
        pltpu.make_async_copy(gates_h, gates, sem_l.at[5]),
    ]
    for cp in loc:
        cp.start()
    pl.semaphore_wait(barrier, 5 + mid)
    loc[0].wait()

    def send_z(nb, k, i, h):
        blk = xd.at[k, i, :, span(h)]
        dst = xd.at[k ^ nb, i, :, span(h)]
        return rdma(blk, dst, s_z.at[nb // 2, k, i, h], r_x.at[k ^ nb, i, h], zs[nb] * SIDE + j, c)

    def send_al(k, h):
        return rdma(
            xd.at[k, 0, :, span(h)], xd.at[k, 1, :, span(h)], s_al.at[k, h], r_x.at[k, 1, h], pa, c
        )

    def landed(k, i, h):
        blk = xd.at[k, i, :, span(h)]
        return rdma(blk, blk, s_al.at[k, h], r_x.at[k, i, h], pa, c)

    groups = (gb, gd, ga)

    def send_b(k, i, h, to=None):
        return rdma(
            sb.at[k, i, :, span(h)], xc.at[c, k, groups[i], :, span(h)],
            s_b.at[k, i, h], r_b.at[k, i, h], pb if to is None else to, c,
        )

    def send_c(k, g):
        blk = xc.at[c, k, g]
        return rdma(blk, blk, s_c.at[k, g], r_c.at[k, g], me, oc)

    def table_z(nb, k, i):
        to = zs[nb] * SIDE + j
        return rdma(wbuf.at[k, i], wbuf.at[k ^ nb, i], s_w.at[nb // 2, k, i], r_w.at[k ^ nb, i], to, c)

    def table_al(k):
        return rdma(wbuf.at[k, 0], wbuf.at[k, 1], s_w.at[2, k, 0], r_w.at[k, 1], pa, c)

    def table_landed(k, i):
        return rdma(wbuf.at[k, i], wbuf.at[k, i], s_w.at[2, k, 0], r_w.at[k, i], pa, c)

    send_d = rdma(wd_h.at[0, :, cols(oc)], wd.at[c], s_d, r_d, me, oc)

    def send_h(k):
        blk = hid.at[k, c]
        return rdma(blk, blk, s_h.at[k], r_h.at[k], me, oc)

    def ret_b(k, i, h, to=None):
        return rdma(
            con.at[k, groups[i], :, span(h)], rb.at[k, i, :, span(h)],
            s_rb.at[k, i, h], r_rb.at[k, i, h], pb if to is None else to, c,
        )

    def ret_a(k, h):
        return rdma(
            dd.at[k, 1, :, span(h)], ra.at[k, :, span(h)], s_ra.at[k, h], r_ra.at[k, h], pa, c
        )

    def ret_z(nb, k, i, h):
        slot = LANDING[nb, k ^ nb]
        return rdma(
            dd.at[k, i, :, span(h)], rz.at[slot, i, :, span(h)],
            s_rz.at[k, i, h], r_rz.at[slot, i, h], zs[nb] * SIDE + j, c,
        )

    def summed(slot, i, h):
        blk = rz.at[slot, i, :, span(h)]
        return rdma(blk, blk, s_rz.at[0, i, h], r_rz.at[slot, i, h], pa, c)

    def tabulate():
        row_of = lax.broadcasted_iota(jnp.int32, (n, rows), 0)
        spread = jnp.zeros((n, rows), F32)
        for t in range(ids.shape[0]):
            spread = spread + jnp.where(ids[t : t + 1] == row_of, gates[t : t + 1], 0.0)
        wbuf[0, 0] = spread

    def place(k, i, experts):
        w = wbuf[k, i]
        routed = jnp.where(w > 0.0, 1.0, 0.0)
        first = lax.broadcasted_iota(jnp.int32, (rows, rows), 0)
        second = lax.broadcasted_iota(jnp.int32, (rows, rows), 1)
        rank = jnp.dot(
            routed.astype(bf), jnp.where(first < second, 1.0, 0.0).astype(bf),
            preferred_element_type=F32,
        )
        rank = jnp.where(w > 0.0, rank, -1.0)
        row_of = lax.broadcasted_iota(jnp.int32, (n, rows), 0)
        slot = lax.broadcasted_iota(jnp.int32, (cap, rows), 0).astype(F32)
        slot_t = lax.broadcasted_iota(jnp.int32, (rows, cap), 1).astype(F32)
        picked = []
        for q, e in enumerate(experts):
            keep = row_of == e
            at = jnp.sum(jnp.where(keep, rank, 0.0), axis=0, keepdims=True)
            gate = jnp.sum(jnp.where(keep, w, 0.0), axis=0, keepdims=True)
            picked.append(jnp.where(slot == at, 1.0, 0.0))
            at_t = jnp.sum(jnp.where(first == second, at, 0.0), axis=1, keepdims=True)
            gate_t = jnp.sum(jnp.where(first == second, gate, 0.0), axis=1, keepdims=True)
            pt[k, i, q] = jnp.where(slot_t == at_t, 1.0, 0.0).astype(bf)
            gc[k, i, q] = jnp.broadcast_to(gate_t, (rows, 128))
        pk[k, i, : len(picked) * cap] = jnp.concatenate(picked, axis=0).astype(bf)

    class Role:
        def __init__(self, name):
            self.name = name
            self.other = {1: MID if name == END else END, 3: MID}
            self.nbs = (1,) if name == END else (1, 3)
            self.seen = set()

        def once(self, key, copy):
            if key not in self.seen:
                self.seen.add(key)
                copy.wait_recv()

        def forwards(self, k, i, h):
            found = []
            for nb in self.nbs:
                to = k ^ nb
                if to == 0 or (self.other[nb] == MID and nb == 1 and k != 0):
                    continue
                if nb == 3 and k not in (0, 1) or nb == 1 and self.name == MID and k == 1:
                    continue
                if i == 0 or FETCH[self.other[nb]][to][h] == "z":
                    found.append(nb)
            return found

        def along(self, k, h):
            return FETCH[self.name][k][h] == "a"

        def beside(self, k, h):
            return GIVE[self.name][k][h] == "a"

        def direct(self, k):
            return FETCH[self.name][k][0] == "d"

        def peers(self, k):
            return (pb, pd, pa) if self.direct(k) else (pb, pb)

        def get(self, k, i, h):
            if (k, i, h) in self.seen:
                return
            self.seen.add((k, i, h))
            if (k, i) != (0, 0):
                landed(k, i, h).wait_recv()
            for nb in self.forwards(k, i, h):
                send_z(nb, k, i, h).start()
            if i == 0 and self.along(k, h):
                send_al(k, h).start()
            if h == 0:
                if (k, i) == (0, 0):
                    loc[1].wait()
                    loc[5].wait()
                    tabulate()
                else:
                    table_landed(k, i).wait_recv()
                for nb in self.forwards(k, i, 0):
                    table_z(nb, k, i).start()
                if i == 0 and self.along(k, 0):
                    table_al(k).start()

        def compact(self, k, i, h):
            experts = (me, pb, pd, pa) if self.direct(k) else (me, pb)
            g = 0 if i == 0 else ga
            self.get(k, i, h)
            if ("place", k, i) not in self.seen:
                self.seen.add(("place", k, i))
                self.get(k, i, 0)
                place(k, i, experts)
            at = span(h)
            o = jnp.dot(pk[k, i, : len(experts) * cap], xd[k, i, :, at], preferred_element_type=F32)
            xc[c, k, g, :, at] = o[:cap].astype(bf)
            for q, to in enumerate(experts[1:]):
                sb[k, i + q, :, at] = o[(q + 1) * cap : (q + 2) * cap].astype(bf)
                send_b(k, i + q, h, to).start()
            self.seen.add(("cut", k, i, h))
            if all(("cut", k, i, p) in self.seen for p in parts):
                send_c(k, g).start()

        def relay(self, k, i):
            for h in parts:
                send_b(k, i, h).wait_recv()
            send_c(k, groups[i]).start()

        def up(self, k):
            if "up" not in self.seen:
                self.seen.add("up")
                loc[2].wait()
                loc[3].wait()
            for g in range(4):
                self.once(("c", k, g), send_c(k, g))
            step = min(256, width)

            @pl.loop(0, width // step)
            def _(t):
                at = pl.ds(pl.multiple_of(t * step, step), step)
                x0 = xc[0, k].reshape(SIDE * cap, half)
                x1 = xc[1, k].reshape(SIDE * cap, half)
                g = jnp.dot(x0, wg[:half, at], preferred_element_type=F32)
                g = g + jnp.dot(x1, wg[half:, at], preferred_element_type=F32)
                u = jnp.dot(x0, wu[:half, at], preferred_element_type=F32)
                u = u + jnp.dot(x1, wu[half:, at], preferred_element_type=F32)
                hid[k, c, :, at] = (g / (1.0 + jnp.exp(-g)) * u).astype(bf)

            send_h(k).start()

        def down(self, k, h):
            if "down" not in self.seen:
                self.seen.add("down")
                loc[4].wait()
                send_d.wait_recv()
            if ("h", k) not in self.seen:
                self.once(("h", k), send_h(k))
            at = span(h)

            o = jnp.dot(hid[k, 0], wd[0, :, at], preferred_element_type=F32)
            o = o + jnp.dot(hid[k, 1], wd[1, :, at], preferred_element_type=F32)
            con[k, :, :, at] = o.reshape(SIDE, cap, at.size).astype(bf)

        def give(self, k, i, h):
            ret_b(k, i, h, self.peers(k)[i]).start()

        def incoming(self, k, i, h):
            slots = []
            for nb in self.nbs:
                if (nb, k) in LANDING and not (self.name == END and k != 0):
                    if i == 0 or GIVE[self.other[nb]][k ^ nb][h] == "z":
                        slots.append(LANDING[nb, k])
            return slots

        def toward(self, k):
            return 1 if self.name == END or k == 1 else 3

        def back(self, k, i, h):
            direct = self.direct(k)
            g = 0 if i == 0 else ga
            slots = self.incoming(k, i, h)
            others = range(3) if direct else (i,)
            for q in others:
                ret_b(k, q, h).wait_recv()
            for s in slots:
                summed(s, i, h).wait_recv()
            if i == 0 and self.beside(k, h):
                ret_a(k, h).wait_recv()
            at = span(h)
            o = jnp.dot(pt[k, i, 0], con[k, g, :, at], preferred_element_type=F32) * gc[k, i, 0, :, 0:1]
            for q in others:
                e = q - i + 1
                p = jnp.dot(pt[k, i, e], rb[k, q, :, at], preferred_element_type=F32)
                o = o + p * gc[k, i, e, :, 0:1]
            for s in slots:
                o = o + rz[s, i, :, at].astype(F32)
            if i == 0 and self.beside(k, h):
                o = o + ra[k, :, at].astype(F32)
            if (k, i) == (0, 0):
                out[:, at] = o.astype(bf)
                return
            dd[k, i, :, at] = o.astype(bf)
            if i == 1 and self.beside(k, h):
                ret_a(k, h).start()
            else:
                ret_z(self.toward(k), k, i, h).start()

        def finish(self):
            send_d.wait_send()
            for k in range(PLANES):
                for g in range(4):
                    send_c(k, g).wait_send()
                send_h(k).wait_send()
                if self.along(k, 0):
                    table_al(k).wait_send()
                for i in range(2):
                    for nb in self.forwards(k, i, 0):
                        table_z(nb, k, i).wait_send()
                for h in parts:
                    for i in range(len(self.peers(k))):
                        send_b(k, i, h).wait_send()
                        ret_b(k, i, h).wait_send()
                    if self.along(k, h):
                        send_al(k, h).wait_send()
                    if self.beside(k, h):
                        ret_a(k, h).wait_send()
                    for i in range(2):
                        for nb in self.forwards(k, i, h):
                            send_z(nb, k, i, h).wait_send()
                        if k > 0 and (i == 0 or GIVE[self.name][k][h] == "z"):
                            ret_z(self.toward(k), k, i, h).wait_send()

        def run(self, plan):
            for h in parts:
                self.get(0, 0, h)
            send_d.start()
            steps = (self.get, self.compact, self.relay, self.up, self.down, self.give, self.back)
            for what, *at in plan:
                steps[what](*at)
            self.finish()

    @pl.when(mid == 0)
    def _():
        Role(END).run(PLAN[END])

    @pl.when(mid == 1)
    def _():
        Role(MID).run(PLAN[MID])


PLAN = {
    END: (
        (COMPACT, 0, 0, 0), (COMPACT, 0, 0, 1), (COMPACT, 1, 0, 0), (COMPACT, 0, 0, 2),
        (COMPACT, 1, 0, 1), (COMPACT, 1, 0, 2), (COMPACT, 0, 1, 2), (COMPACT, 1, 1, 1),
        (COMPACT, 1, 1, 0), (COMPACT, 1, 1, 2), (COMPACT, 2, 0, 1), (RELAY, 1, 1),
        (RELAY, 1, 0), (COMPACT, 3, 0, 0), (COMPACT, 3, 0, 2), (UP, 1),
        (COMPACT, 3, 0, 1), (COMPACT, 3, 1, 0), (COMPACT, 3, 1, 2), (COMPACT, 3, 1, 1),
        (DOWN, 1, 2), (RELAY, 3, 0), (RELAY, 0, 0), (GIVE_BACK, 1, 1, 2),
        (DOWN, 1, 1), (DOWN, 1, 0), (GIVE_BACK, 1, 1, 1), (COMPACT, 2, 1, 1),
        (GIVE_BACK, 1, 0, 1), (RELAY, 3, 1), (COMPACT, 2, 0, 2), (COMPACT, 2, 0, 0),
        (COMPACT, 2, 1, 0), (BACK, 1, 1, 2), (COMPACT, 2, 1, 2), (GIVE_BACK, 1, 1, 0),
        (UP, 3), (COMPACT, 0, 1, 0), (RELAY, 2, 0), (BACK, 1, 1, 1),
        (BACK, 1, 0, 1), (COMPACT, 0, 1, 1), (RELAY, 2, 1), (DOWN, 3, 1),
        (GIVE_BACK, 3, 0, 1), (DOWN, 3, 0), (GIVE_BACK, 3, 1, 0), (DOWN, 3, 2),
        (GIVE_BACK, 3, 1, 1), (GIVE_BACK, 3, 0, 0), (GIVE_BACK, 3, 0, 2), (UP, 2),
        (GIVE_BACK, 3, 1, 2), (BACK, 3, 0, 1), (BACK, 3, 1, 0), (BACK, 3, 1, 1),
        (DOWN, 2, 1), (GIVE_BACK, 2, 1, 1), (RELAY, 0, 1), (BACK, 3, 1, 2),
        (DOWN, 2, 0), (GIVE_BACK, 2, 0, 1), (GIVE_BACK, 2, 1, 0), (DOWN, 2, 2),
        (BACK, 3, 0, 0), (GIVE_BACK, 2, 0, 0), (BACK, 2, 1, 1), (UP, 0),
        (GIVE_BACK, 2, 1, 2), (BACK, 3, 0, 2), (BACK, 2, 1, 0), (BACK, 2, 0, 1),
        (DOWN, 0, 1), (GIVE_BACK, 2, 0, 2), (GIVE_BACK, 1, 0, 0), (BACK, 2, 1, 2),
        (BACK, 2, 0, 0), (DOWN, 0, 2), (GIVE_BACK, 0, 1, 1), (BACK, 1, 1, 0),
        (BACK, 2, 0, 2), (GIVE_BACK, 0, 1, 2), (DOWN, 0, 0), (GIVE_BACK, 0, 1, 0),
        (GIVE_BACK, 0, 0, 2), (BACK, 0, 1, 1), (BACK, 1, 0, 0), (GIVE_BACK, 1, 0, 2),
        (BACK, 0, 1, 0), (GIVE_BACK, 0, 0, 1), (GIVE_BACK, 0, 0, 0), (BACK, 0, 1, 2),
        (BACK, 1, 0, 2), (BACK, 0, 0, 1), (BACK, 0, 0, 0), (BACK, 0, 0, 2),
    ),
    MID: (
        (COMPACT, 0, 0, 2), (COMPACT, 0, 0, 0), (COMPACT, 1, 0, 0), (COMPACT, 3, 0, 1),
        (COMPACT, 1, 0, 2), (COMPACT, 1, 0, 1), (COMPACT, 2, 0, 0), (GET, 3, 0, 0),
        (COMPACT, 1, 1, 0), (COMPACT, 1, 1, 1), (COMPACT, 1, 1, 2), (COMPACT, 2, 0, 2),
        (COMPACT, 0, 0, 1), (COMPACT, 2, 0, 1), (COMPACT, 3, 0, 0), (COMPACT, 0, 1, 2),
        (GET, 0, 1, 0), (RELAY, 1, 0), (RELAY, 1, 1), (COMPACT, 2, 1, 1),
        (COMPACT, 3, 0, 2), (COMPACT, 2, 1, 0), (UP, 1), (COMPACT, 2, 1, 2),
        (COMPACT, 0, 1, 1), (GET, 3, 1, 2), (COMPACT, 0, 1, 0), (COMPACT, 3, 1, 2),
        (DOWN, 1, 2), (DOWN, 1, 1), (COMPACT, 3, 1, 0), (RELAY, 2, 0),
        (RELAY, 2, 1), (RELAY, 0, 0), (RELAY, 0, 1), (GIVE_BACK, 1, 0, 1),
        (COMPACT, 3, 1, 1), (DOWN, 1, 0), (RELAY, 3, 0), (GIVE_BACK, 1, 1, 1),
        (UP, 2), (UP, 0), (GIVE_BACK, 1, 1, 0), (DOWN, 2, 0),
        (GIVE_BACK, 1, 1, 2), (DOWN, 2, 2), (GIVE_BACK, 2, 1, 2), (GIVE_BACK, 1, 0, 0),
        (RELAY, 3, 1), (GIVE_BACK, 2, 1, 0), (DOWN, 0, 0), (DOWN, 2, 1),
        (GIVE_BACK, 2, 0, 2), (GIVE_BACK, 2, 1, 1), (GIVE_BACK, 1, 0, 2), (DOWN, 0, 1),
        (GIVE_BACK, 0, 1, 0), (UP, 3), (GIVE_BACK, 2, 0, 1), (BACK, 2, 1, 0),
        (GIVE_BACK, 2, 0, 0), (GIVE_BACK, 0, 0, 0), (DOWN, 3, 0), (GIVE_BACK, 3, 1, 0),
        (GIVE_BACK, 0, 1, 1), (BACK, 2, 0, 1), (BACK, 2, 1, 2), (DOWN, 3, 1),
        (GIVE_BACK, 3, 1, 1), (DOWN, 3, 2), (BACK, 1, 1, 2), (BACK, 2, 1, 1),
        (BACK, 3, 1, 0), (BACK, 1, 1, 0), (GIVE_BACK, 3, 0, 1), (GIVE_BACK, 3, 1, 2),
        (BACK, 2, 0, 0), (GIVE_BACK, 3, 0, 0), (DOWN, 0, 2), (BACK, 3, 1, 1),
        (BACK, 0, 1, 1), (GIVE_BACK, 0, 1, 2), (BACK, 1, 1, 1), (BACK, 1, 0, 1),
        (BACK, 2, 0, 2), (GIVE_BACK, 3, 0, 2), (BACK, 3, 1, 2), (GIVE_BACK, 0, 0, 2),
        (BACK, 0, 1, 0), (BACK, 3, 0, 1), (BACK, 1, 0, 0), (GIVE_BACK, 0, 0, 1),
        (BACK, 0, 1, 2), (BACK, 3, 0, 0), (BACK, 1, 0, 2), (BACK, 3, 0, 2),
        (BACK, 0, 0, 0), (BACK, 0, 0, 1), (BACK, 0, 0, 2),
    ),
}


def plane_shards(tokens, expert_ids, routing_gates, w_gate, w_up, w_down):
    n = PLANES * SIDE
    rows, model_width = tokens.shape
    half = model_width // 2
    width = w_gate.shape[2]
    topk = expert_ids.shape[1]
    cap = rows * topk * 9 // (8 * n)
    bf = jnp.bfloat16
    dma = pltpu.SemaphoreType.DMA
    anyspec = pl.BlockSpec(memory_space=pl.ANY)
    return pl.pallas_call(
        kernel,
        out_shape=pltpu.VMEM((rows, half), bf),
        in_specs=[anyspec] * 6,
        out_specs=pl.BlockSpec(memory_space=pltpu.VMEM),
        scratch_shapes=[
            pltpu.VMEM((PLANES, 2, rows, half), bf),
            pltpu.VMEM((2, PLANES, SIDE, cap, half), bf),
            pltpu.VMEM((PLANES, 3, cap, half), bf),
            pltpu.VMEM((PLANES, 2, SIDE * cap, rows), bf),
            pltpu.VMEM((PLANES, 2, SIDE, rows, cap), bf),
            pltpu.VMEM((PLANES, 2, SIDE, rows, 128), F32),
            pltpu.VMEM((topk, rows), jnp.int32),
            pltpu.VMEM((topk, rows), F32),
            pltpu.VMEM((PLANES, 2, n, rows), F32),
            pltpu.VMEM((model_width, width), bf),
            pltpu.VMEM((model_width, width), bf),
            pltpu.VMEM((2, width, half), bf),
            pltpu.VMEM((PLANES, 2, SIDE * cap, width), bf),
            pltpu.VMEM((PLANES, SIDE, cap, half), bf),
            pltpu.VMEM((PLANES, 3, cap, half), bf),
            pltpu.VMEM((PLANES, 2, rows, half), bf),
            pltpu.VMEM((PLANES, rows, half), bf),
            pltpu.VMEM((len(LANDING), 2, rows, half), bf),
            dma((6,)),
            dma((2, PLANES, 2, PARTS)), dma((PLANES, PARTS)), dma((PLANES, 2, PARTS)),
            dma((PLANES, 3, PARTS)), dma((PLANES, 3, PARTS)),
            dma((PLANES, SIDE)), dma((PLANES, SIDE)),
            dma((PLANES,)), dma((PLANES,)),
            dma, dma,
            dma((3, PLANES, 2)), dma((PLANES, 2)),
            dma((PLANES, 3, PARTS)), dma((PLANES, 3, PARTS)),
            dma((PLANES, PARTS)), dma((PLANES, PARTS)),
            dma((PLANES, 2, PARTS)), dma((len(LANDING), 2, PARTS)),
        ],
        compiler_params=pltpu.CompilerParams(
            collective_id=0, has_side_effects=True, vmem_limit_bytes=60 << 20
        ),
        cost_estimate=pl.CostEstimate(
            flops=6 * n * cap * model_width * width, bytes_accessed=12 << 20,
            transcendentals=n * cap * width,
        ),
        name="planes",
    )(tokens, expert_ids.T, routing_gates.T, w_gate, w_up, w_down)


def solution(mesh):
    small = mesh.shape["ep"] == PLANES * SIDE and mesh.shape["etp"] == 2
    return jax.shard_map(
        plane_shards if small else plain_shards,
        mesh=mesh,
        in_specs=(
            P("ep", None),
            P("ep", None),
            P("ep", None),
            P("ep", None, "etp"),
            P("ep", None, "etp"),
            P("ep", "etp", None),
        ),
        out_specs=P("ep", "etp"),
        check_vma=False,
    )
```

```python
import functools

import jax
import jax.numpy as jnp
from jax import lax
from jax.experimental import pallas as pl
from jax.experimental.pallas import tpu as pltpu
from jax.sharding import PartitionSpec as P

MESH = pl.DeviceIdType.MESH
F32 = jnp.float32
PLANES = 4
SIDE = 4
PARTS = 3
END, MID = 0, 1
GET, COMPACT, RELAY, UP, DOWN, GIVE_BACK, BACK = range(7)
FETCH = {
    END: {0: "aaa", 1: "aaa", 2: "azz", 3: "aaz"},
    MID: {0: "aaa", 1: "zzz", 2: "aaa", 3: "aaz"},
}
GIVE = {
    END: {0: "aaa", 1: "azz", 2: "aaa", 3: "aza"},
    MID: {0: "aaa", 1: "zzz", 2: "zza", 3: "aaa"},
}
LANDING = {(1, 0): 0, (1, 2): 1, (1, 3): 2, (3, 0): 3, (3, 1): 4}


def plain_shards(tokens, expert_ids, routing_gates, w_gate, w_up, w_down):
    ep_count = lax.axis_size("ep")
    tok_rows, topk_count = expert_ids.shape
    model_width = tokens.shape[1]
    half_width = model_width // lax.axis_size("etp")
    capacity = max(2, tok_rows * topk_count * 9 // (8 * ep_count))
    flat_ids = expert_ids.reshape(-1)
    onehot = (flat_ids[:, None] == jnp.arange(ep_count, dtype=jnp.int32)[None, :]).astype(jnp.bfloat16)
    row_range = jnp.arange(tok_rows * topk_count, dtype=jnp.int32)
    earlier = (row_range[None, :] < row_range[:, None]).astype(jnp.bfloat16)
    counted = jnp.dot(earlier, onehot, preferred_element_type=F32)
    row_ranks = jnp.sum(counted * onehot.astype(F32), axis=1).astype(jnp.int32)
    slot_index = flat_ids * capacity + row_ranks
    slot_table = slot_index.reshape(tok_rows, topk_count)
    slot_range = jnp.arange(ep_count * capacity, dtype=jnp.int32)
    dispatch = jnp.any(slot_range[:, None, None] == slot_table[None, :, :], axis=2).astype(
        jnp.bfloat16
    )
    outgoing = jnp.dot(dispatch, tokens, preferred_element_type=jnp.float32).astype(jnp.bfloat16)
    outgoing = outgoing.reshape(ep_count, capacity, model_width)
    arrived = lax.all_to_all(outgoing, "ep", split_axis=0, concat_axis=0, tiled=True)
    expert_rows = arrived.reshape(ep_count * capacity, model_width)
    gate_val = jnp.dot(expert_rows, w_gate[0], preferred_element_type=jnp.float32)
    up_val = jnp.dot(expert_rows, w_up[0], preferred_element_type=jnp.float32)
    hidden = (jax.nn.silu(gate_val) * up_val).astype(jnp.bfloat16)
    partial_value = jnp.dot(hidden, w_down[0], preferred_element_type=jnp.float32)
    summed = lax.psum_scatter(
        partial_value.astype(jnp.bfloat16), "etp", scatter_dimension=1, tiled=True
    )
    outgoing_back = summed.reshape(ep_count, capacity, half_width)
    returned = lax.all_to_all(outgoing_back, "ep", split_axis=0, concat_axis=0, tiled=True).reshape(
        -1, half_width
    )
    picked = returned[slot_index].reshape(tok_rows, topk_count, half_width).astype(jnp.float32)
    combined = jnp.einsum("tk,tkd->td", routing_gates, picked)
    return combined.astype(jnp.bfloat16)


def kernel(
    tok, ids_h, gates_h, wg_h, wu_h, wd_h, out,
    xd, xc, sb, pk, pt, gc, ids, gates, wbuf, wg, wu, wd, hid, con, rb, dd, ra, rz,
    sem_l, s_z, s_al, r_x, s_b, r_b, s_c, r_c, s_h, r_h, s_d, r_d, s_w, r_w,
    s_rb, r_rb, s_ra, r_ra, s_rz, r_rz,
):
    me, c = lax.axis_index("ep"), lax.axis_index("etp")
    n = PLANES * SIDE
    oc = 1 - c
    x, y, z = me % 2, (me // 2) % 2, me // 4
    j = me % 4
    xj, yj = j + 1 - 2 * x, j + 2 - 4 * y
    ja = xj + c * (yj - xj)
    jb = yj + c * (xj - yj)
    pa, pb, pd = me - j + ja, me - j + jb, me - j + xj + yj - j
    ga, gb, gd = 1 + c, 2 - c, 3
    z1, z2, z3 = z + 1 - 2 * (z % 2), z + 2 - 4 * (z // 2), 3 - z
    zs = [z, z1, z2, z3]
    mid = (z % 2 + z // 2) % 2
    rows, half = out.shape
    width = wg.shape[1]
    cap = sb.shape[2]
    bf = jnp.bfloat16
    tile = 256
    tiles = half // tile
    cuts = [(p * tiles + PARTS - 1) // PARTS for p in range(PARTS + 1)]
    parts = range(PARTS)

    def span(h):
        return pl.ds(cuts[h] * tile, (cuts[h + 1] - cuts[h]) * tile)

    def rdma(src, dst, ss, rs, ep, core):
        return pltpu.make_async_remote_copy(
            src_ref=src, dst_ref=dst, send_sem=ss, recv_sem=rs,
            device_id=(ep, core), device_id_type=MESH,
        )

    barrier = pltpu.get_barrier_semaphore()

    def greet(ep, core):
        pl.semaphore_signal(barrier, inc=1, device_id=(ep, core), device_id_type=MESH)

    for peer in (z1 * SIDE + j, pa, pb, pd):
        greet(peer, c)
    greet(me, oc)
    pl.when(mid == 1)(lambda: greet(z3 * SIDE + j, c))

    def cols(k):
        return pl.ds(pl.multiple_of(k * half, 128), half)

    loc = [
        pltpu.make_async_copy(tok.at[:, cols(c)], xd.at[0, 0], sem_l.at[0]),
        pltpu.make_async_copy(ids_h, ids, sem_l.at[1]),
        pltpu.make_async_copy(wg_h.at[0], wg, sem_l.at[2]),
        pltpu.make_async_copy(wu_h.at[0], wu, sem_l.at[3]),
        pltpu.make_async_copy(wd_h.at[0, :, cols(c)], wd.at[c], sem_l.at[4]),
        pltpu.make_async_copy(gates_h, gates, sem_l.at[5]),
    ]
    for p in (0, 1, 5, 2, 3, 4):
        loc[p].start()
    pl.semaphore_wait(barrier, 5 + mid)
    loc[0].wait()

    def send_z(nb, k, i, h):
        blk = xd.at[k, i, :, span(h)]
        dst = xd.at[k ^ nb, i, :, span(h)]
        return rdma(blk, dst, s_z.at[nb // 2, k, i, h], r_x.at[k ^ nb, i, h], zs[nb] * SIDE + j, c)

    def send_al(k, h):
        return rdma(
            xd.at[k, 0, :, span(h)], xd.at[k, 1, :, span(h)], s_al.at[k, h], r_x.at[k, 1, h], pa, c
        )

    def landed(k, i, h):
        blk = xd.at[k, i, :, span(h)]
        return rdma(blk, blk, s_al.at[k, h], r_x.at[k, i, h], pa, c)

    groups = (gb, gd, ga)

    def send_b(k, i, h, to=None):
        return rdma(
            sb.at[k, i, :, span(h)], xc.at[c, k, groups[i], :, span(h)],
            s_b.at[k, i, h], r_b.at[k, i, h], pb if to is None else to, c,
        )

    def send_c(k, g):
        blk = xc.at[c, k, g]
        return rdma(blk, blk, s_c.at[k, g], r_c.at[k, g], me, oc)

    def table_z(nb, k, i):
        to = zs[nb] * SIDE + j
        return rdma(wbuf.at[k, i], wbuf.at[k ^ nb, i], s_w.at[nb // 2, k, i], r_w.at[k ^ nb, i], to, c)

    def table_al(k):
        return rdma(wbuf.at[k, 0], wbuf.at[k, 1], s_w.at[2, k, 0], r_w.at[k, 1], pa, c)

    def table_landed(k, i):
        return rdma(wbuf.at[k, i], wbuf.at[k, i], s_w.at[2, k, 0], r_w.at[k, i], pa, c)

    send_d = rdma(wd_h.at[0, :, cols(oc)], wd.at[c], s_d, r_d, me, oc)

    def send_h(k):
        blk = hid.at[k, c]
        return rdma(blk, blk, s_h.at[k], r_h.at[k], me, oc)

    def ret_b(k, i, h, to=None):
        return rdma(
            con.at[k, groups[i], :, span(h)], rb.at[k, i, :, span(h)],
            s_rb.at[k, i, h], r_rb.at[k, i, h], pb if to is None else to, c,
        )

    def ret_a(k, h):
        return rdma(
            dd.at[k, 1, :, span(h)], ra.at[k, :, span(h)], s_ra.at[k, h], r_ra.at[k, h], pa, c
        )

    def ret_z(nb, k, i, h):
        slot = LANDING[nb, k ^ nb]
        return rdma(
            dd.at[k, i, :, span(h)], rz.at[slot, i, :, span(h)],
            s_rz.at[k, i, h], r_rz.at[slot, i, h], zs[nb] * SIDE + j, c,
        )

    def summed(slot, i, h):
        blk = rz.at[slot, i, :, span(h)]
        return rdma(blk, blk, s_rz.at[0, i, h], r_rz.at[slot, i, h], pa, c)

    def tabulate():
        row_of = lax.broadcasted_iota(jnp.int32, (n, rows), 0)
        spread = jnp.zeros((n, rows), F32)
        for t in range(ids.shape[0]):
            spread = spread + jnp.where(ids[t : t + 1] == row_of, gates[t : t + 1], 0.0)
        wbuf[0, 0] = spread

    def place(k, i, experts):
        w = wbuf[k, i]
        routed = jnp.where(w > 0.0, 1.0, 0.0)
        first = lax.broadcasted_iota(jnp.int32, (rows, rows), 0)
        second = lax.broadcasted_iota(jnp.int32, (rows, rows), 1)
        rank = jnp.dot(
            routed.astype(bf), jnp.where(first < second, 1.0, 0.0).astype(bf),
            preferred_element_type=F32,
        )
        rank = jnp.where(w > 0.0, rank, -1.0)
        row_of = lax.broadcasted_iota(jnp.int32, (n, rows), 0)
        slot = lax.broadcasted_iota(jnp.int32, (cap, rows), 0).astype(F32)
        slot_t = lax.broadcasted_iota(jnp.int32, (rows, cap), 1).astype(F32)
        picked = []
        for q, e in enumerate(experts):
            keep = row_of == e
            at = jnp.sum(jnp.where(keep, rank, 0.0), axis=0, keepdims=True)
            gate = jnp.sum(jnp.where(keep, w, 0.0), axis=0, keepdims=True)
            picked.append(jnp.where(slot == at, 1.0, 0.0))
            at_t = jnp.sum(jnp.where(first == second, at, 0.0), axis=1, keepdims=True)
            gate_t = jnp.sum(jnp.where(first == second, gate, 0.0), axis=1, keepdims=True)
            pt[k, i, q] = jnp.where(slot_t == at_t, 1.0, 0.0).astype(bf)
            gc[k, i, q] = jnp.broadcast_to(gate_t, (rows, 128))
        pk[k, i, : len(picked) * cap] = jnp.concatenate(picked, axis=0).astype(bf)

    class Role:
        def __init__(self, name):
            self.name = name
            self.other = {1: MID if name == END else END, 3: MID}
            self.nbs = (1,) if name == END else (1, 3)
            self.seen = set()

        def once(self, key, copy):
            if key not in self.seen:
                self.seen.add(key)
                copy.wait_recv()

        def forwards(self, k, i, h):
            found = []
            for nb in self.nbs:
                to = k ^ nb
                if to == 0 or (self.other[nb] == MID and nb == 1 and k != 0):
                    continue
                if nb == 3 and k not in (0, 1) or nb == 1 and self.name == MID and k == 1:
                    continue
                if i == 0 or FETCH[self.other[nb]][to][h] == "z":
                    found.append(nb)
            return found

        def along(self, k, h):
            return FETCH[self.name][k][h] == "a"

        def beside(self, k, h):
            return GIVE[self.name][k][h] == "a"

        def direct(self, k):
            return FETCH[self.name][k][0] == "d"

        def peers(self, k):
            return (pb, pd, pa) if self.direct(k) else (pb, pb)

        def get(self, k, i, h):
            if (k, i, h) in self.seen:
                return
            self.seen.add((k, i, h))
            if (k, i) != (0, 0):
                landed(k, i, h).wait_recv()
            for nb in self.forwards(k, i, h):
                send_z(nb, k, i, h).start()
            if i == 0 and self.along(k, h):
                send_al(k, h).start()
            if h == 0:
                if (k, i) == (0, 0):
                    loc[1].wait()
                    loc[5].wait()
                    tabulate()
                else:
                    table_landed(k, i).wait_recv()
                for nb in self.forwards(k, i, 0):
                    table_z(nb, k, i).start()
                if i == 0 and self.along(k, 0):
                    table_al(k).start()

        def compact(self, k, i, h):
            experts = (me, pb, pd, pa) if self.direct(k) else (me, pb)
            g = 0 if i == 0 else ga
            self.get(k, i, h)
            if ("place", k, i) not in self.seen:
                self.seen.add(("place", k, i))
                self.get(k, i, 0)
                place(k, i, experts)
            at = span(h)
            o = jnp.dot(pk[k, i, : len(experts) * cap], xd[k, i, :, at], preferred_element_type=F32)
            xc[c, k, g, :, at] = o[:cap].astype(bf)
            for q, to in enumerate(experts[1:]):
                sb[k, i + q, :, at] = o[(q + 1) * cap : (q + 2) * cap].astype(bf)
                send_b(k, i + q, h, to).start()
            self.seen.add(("cut", k, i, h))
            if all(("cut", k, i, p) in self.seen for p in parts):
                send_c(k, g).start()

        def relay(self, k, i):
            for h in parts:
                send_b(k, i, h).wait_recv()
            send_c(k, groups[i]).start()

        def up(self, k):
            if "up" not in self.seen:
                self.seen.add("up")
                loc[2].wait()
                loc[3].wait()
            for g in range(4):
                self.once(("c", k, g), send_c(k, g))
            step = min(256, width)

            @pl.loop(0, width // step)
            def _(t):
                at = pl.ds(pl.multiple_of(t * step, step), step)
                x0 = xc[0, k].reshape(SIDE * cap, half)
                x1 = xc[1, k].reshape(SIDE * cap, half)
                g = jnp.dot(x0, wg[:half, at], preferred_element_type=F32)
                g = g + jnp.dot(x1, wg[half:, at], preferred_element_type=F32)
                u = jnp.dot(x0, wu[:half, at], preferred_element_type=F32)
                u = u + jnp.dot(x1, wu[half:, at], preferred_element_type=F32)
                hid[k, c, :, at] = (g / (1.0 + jnp.exp(-g)) * u).astype(bf)

            send_h(k).start()

        def down(self, k, h):
            if "down" not in self.seen:
                self.seen.add("down")
                loc[4].wait()
                send_d.wait_recv()
            if ("h", k) not in self.seen:
                self.once(("h", k), send_h(k))
            at = span(h)

            o = jnp.dot(hid[k, 0], wd[0, :, at], preferred_element_type=F32)
            o = o + jnp.dot(hid[k, 1], wd[1, :, at], preferred_element_type=F32)
            con[k, :, :, at] = o.reshape(SIDE, cap, at.size).astype(bf)

        def give(self, k, i, h):
            ret_b(k, i, h, self.peers(k)[i]).start()

        def incoming(self, k, i, h):
            slots = []
            for nb in self.nbs:
                if (nb, k) in LANDING and not (self.name == END and k != 0):
                    if i == 0 or GIVE[self.other[nb]][k ^ nb][h] == "z":
                        slots.append(LANDING[nb, k])
            return slots

        def toward(self, k):
            return 1 if self.name == END or k == 1 else 3

        def back(self, k, i, h):
            direct = self.direct(k)
            g = 0 if i == 0 else ga
            slots = self.incoming(k, i, h)
            others = range(3) if direct else (i,)
            for q in others:
                ret_b(k, q, h).wait_recv()
            for s in slots:
                summed(s, i, h).wait_recv()
            if i == 0 and self.beside(k, h):
                ret_a(k, h).wait_recv()
            at = span(h)
            o = jnp.dot(pt[k, i, 0], con[k, g, :, at], preferred_element_type=F32) * gc[k, i, 0, :, 0:1]
            for q in others:
                e = q - i + 1
                p = jnp.dot(pt[k, i, e], rb[k, q, :, at], preferred_element_type=F32)
                o = o + p * gc[k, i, e, :, 0:1]
            for s in slots:
                o = o + rz[s, i, :, at].astype(F32)
            if i == 0 and self.beside(k, h):
                o = o + ra[k, :, at].astype(F32)
            if (k, i) == (0, 0):
                out[:, at] = o.astype(bf)
                return
            dd[k, i, :, at] = o.astype(bf)
            if i == 1 and self.beside(k, h):
                ret_a(k, h).start()
            else:
                ret_z(self.toward(k), k, i, h).start()

        def finish(self):
            send_d.wait_send()
            for k in range(PLANES):
                for g in range(4):
                    send_c(k, g).wait_send()
                send_h(k).wait_send()
                if self.along(k, 0):
                    table_al(k).wait_send()
                for i in range(2):
                    for nb in self.forwards(k, i, 0):
                        table_z(nb, k, i).wait_send()
                for h in parts:
                    for i in range(len(self.peers(k))):
                        send_b(k, i, h).wait_send()
                        ret_b(k, i, h).wait_send()
                    if self.along(k, h):
                        send_al(k, h).wait_send()
                    if self.beside(k, h):
                        ret_a(k, h).wait_send()
                    for i in range(2):
                        for nb in self.forwards(k, i, h):
                            send_z(nb, k, i, h).wait_send()
                        if k > 0 and (i == 0 or GIVE[self.name][k][h] == "z"):
                            ret_z(self.toward(k), k, i, h).wait_send()

        def run(self, plan):
            for h in parts:
                self.get(0, 0, h)
            send_d.start()
            steps = (self.get, self.compact, self.relay, self.up, self.down, self.give, self.back)
            for what, *at in plan:
                steps[what](*at)
            self.finish()

    @pl.when(mid == 0)
    def _():
        Role(END).run(PLAN[END])

    @pl.when(mid == 1)
    def _():
        Role(MID).run(PLAN[MID])


PLAN = {
    END: (
        (COMPACT, 0, 0, 2), (COMPACT, 0, 0, 0), (COMPACT, 1, 0, 0), (COMPACT, 0, 1, 2),
        (COMPACT, 1, 0, 1), (GET, 0, 1, 0), (COMPACT, 1, 0, 2), (COMPACT, 0, 1, 1),
        (COMPACT, 1, 1, 0), (COMPACT, 1, 1, 1), (COMPACT, 1, 1, 2), (COMPACT, 2, 0, 0),
        (RELAY, 1, 0), (COMPACT, 0, 1, 0), (RELAY, 1, 1), (COMPACT, 3, 0, 0),
        (COMPACT, 3, 0, 1), (UP, 1), (COMPACT, 3, 0, 2), (COMPACT, 3, 1, 0),
        (COMPACT, 3, 1, 1), (COMPACT, 3, 1, 2), (DOWN, 1, 1), (DOWN, 1, 0),
        (GIVE_BACK, 1, 0, 1), (DOWN, 1, 2), (RELAY, 0, 1), (RELAY, 3, 0),
        (GIVE_BACK, 1, 0, 2), (COMPACT, 2, 0, 2), (GIVE_BACK, 1, 1, 1), (RELAY, 3, 1),
        (COMPACT, 2, 0, 1), (GIVE_BACK, 1, 1, 0), (COMPACT, 2, 1, 0), (BACK, 1, 0, 1),
        (COMPACT, 2, 1, 1), (UP, 3), (COMPACT, 2, 1, 2), (BACK, 1, 1, 1),
        (RELAY, 2, 0), (BACK, 1, 0, 2), (GIVE_BACK, 1, 1, 2), (COMPACT, 0, 0, 1),
        (DOWN, 3, 2), (GIVE_BACK, 3, 0, 2), (RELAY, 2, 1), (DOWN, 3, 1),
        (GIVE_BACK, 3, 1, 1), (GIVE_BACK, 3, 0, 1), (BACK, 1, 1, 2), (GIVE_BACK, 3, 1, 2),
        (DOWN, 3, 0), (GIVE_BACK, 3, 1, 0), (GIVE_BACK, 3, 0, 0), (UP, 2),
        (BACK, 3, 1, 1), (BACK, 3, 1, 2), (RELAY, 0, 0), (BACK, 3, 0, 1),
        (BACK, 3, 1, 0), (DOWN, 2, 1), (DOWN, 2, 0), (GIVE_BACK, 2, 1, 0),
        (GIVE_BACK, 2, 1, 1), (DOWN, 2, 2), (GIVE_BACK, 2, 0, 0), (BACK, 3, 0, 2),
        (GIVE_BACK, 2, 1, 2), (BACK, 2, 1, 0), (BACK, 3, 0, 0), (BACK, 1, 1, 0),
        (BACK, 2, 1, 1), (UP, 0), (BACK, 2, 0, 0), (BACK, 2, 1, 2),
        (GIVE_BACK, 2, 0, 1), (GIVE_BACK, 1, 0, 0), (DOWN, 0, 2), (GIVE_BACK, 2, 0, 2),
        (DOWN, 0, 1), (DOWN, 0, 0), (BACK, 2, 0, 1), (GIVE_BACK, 0, 1, 2),
        (GIVE_BACK, 0, 1, 0), (BACK, 2, 0, 2), (GIVE_BACK, 0, 0, 0), (GIVE_BACK, 0, 1, 1),
        (BACK, 0, 1, 2), (GIVE_BACK, 0, 0, 2), (BACK, 0, 1, 0), (BACK, 1, 0, 0),
        (BACK, 0, 1, 1), (GIVE_BACK, 0, 0, 1), (BACK, 0, 0, 1), (BACK, 0, 0, 2),
        (BACK, 0, 0, 0),
    ),
    MID: (
        (COMPACT, 0, 0, 1), (COMPACT, 3, 0, 0), (COMPACT, 1, 0, 0), (COMPACT, 3, 0, 1),
        (COMPACT, 1, 0, 1), (COMPACT, 1, 0, 2), (COMPACT, 2, 0, 0), (COMPACT, 2, 0, 1),
        (COMPACT, 2, 0, 2), (COMPACT, 1, 1, 0), (RELAY, 1, 0), (COMPACT, 1, 1, 2),
        (COMPACT, 2, 1, 0), (COMPACT, 1, 1, 1), (COMPACT, 2, 1, 2), (COMPACT, 2, 1, 1),
        (COMPACT, 0, 1, 2), (COMPACT, 3, 0, 2), (RELAY, 2, 0), (COMPACT, 0, 1, 1),
        (COMPACT, 0, 0, 0), (COMPACT, 0, 0, 2), (RELAY, 1, 1), (COMPACT, 3, 1, 1),
        (RELAY, 2, 1), (UP, 1), (COMPACT, 3, 1, 2), (UP, 2),
        (COMPACT, 0, 1, 0), (COMPACT, 3, 1, 0), (DOWN, 1, 2), (DOWN, 1, 0),
        (DOWN, 2, 2), (DOWN, 2, 0), (DOWN, 2, 1), (RELAY, 3, 0),
        (GIVE_BACK, 2, 1, 0), (RELAY, 3, 1), (GIVE_BACK, 1, 0, 0), (GIVE_BACK, 2, 0, 0),
        (DOWN, 1, 1), (GIVE_BACK, 2, 1, 1), (GIVE_BACK, 2, 0, 1), (GIVE_BACK, 1, 1, 0),
        (GIVE_BACK, 1, 0, 1), (RELAY, 0, 1), (GIVE_BACK, 2, 1, 2), (RELAY, 0, 0),
        (UP, 3), (BACK, 2, 1, 0), (UP, 0), (DOWN, 3, 2),
        (GIVE_BACK, 3, 1, 2), (GIVE_BACK, 2, 0, 2), (GIVE_BACK, 3, 0, 2), (DOWN, 3, 1),
        (DOWN, 3, 0), (GIVE_BACK, 1, 1, 1), (BACK, 2, 1, 2), (BACK, 2, 1, 1),
        (DOWN, 0, 0), (GIVE_BACK, 3, 1, 0), (DOWN, 0, 2), (GIVE_BACK, 3, 1, 1),
        (BACK, 2, 0, 1), (BACK, 1, 1, 0), (GIVE_BACK, 1, 0, 2), (GIVE_BACK, 1, 1, 2),
        (BACK, 3, 1, 0), (DOWN, 0, 1), (BACK, 1, 1, 1), (BACK, 2, 0, 2),
        (BACK, 1, 1, 2), (GIVE_BACK, 3, 0, 0), (GIVE_BACK, 0, 1, 2), (BACK, 3, 1, 1),
        (GIVE_BACK, 0, 0, 1), (GIVE_BACK, 3, 0, 1), (GIVE_BACK, 0, 1, 0), (BACK, 1, 0, 1),
        (BACK, 2, 0, 0), (GIVE_BACK, 0, 1, 1), (GIVE_BACK, 0, 0, 0), (BACK, 1, 0, 2),
        (BACK, 3, 0, 0), (GIVE_BACK, 0, 0, 2), (BACK, 3, 1, 2), (BACK, 1, 0, 0),
        (BACK, 0, 1, 0), (BACK, 3, 0, 1), (BACK, 3, 0, 2), (BACK, 0, 1, 2),
        (BACK, 0, 1, 1), (BACK, 0, 0, 0), (BACK, 0, 0, 1), (BACK, 0, 0, 2),
    ),
}


def plane_shards(tokens, expert_ids, routing_gates, w_gate, w_up, w_down):
    n = PLANES * SIDE
    rows, model_width = tokens.shape
    half = model_width // 2
    width = w_gate.shape[2]
    topk = expert_ids.shape[1]
    cap = rows * topk * 9 // (8 * n)
    bf = jnp.bfloat16
    dma = pltpu.SemaphoreType.DMA
    anyspec = pl.BlockSpec(memory_space=pl.ANY)
    return pl.pallas_call(
        kernel,
        out_shape=pltpu.VMEM((rows, half), bf),
        in_specs=[anyspec] * 6,
        out_specs=pl.BlockSpec(memory_space=pltpu.VMEM),
        scratch_shapes=[
            pltpu.VMEM((PLANES, 2, rows, half), bf),
            pltpu.VMEM((2, PLANES, SIDE, cap, half), bf),
            pltpu.VMEM((PLANES, 3, cap, half), bf),
            pltpu.VMEM((PLANES, 2, SIDE * cap, rows), bf),
            pltpu.VMEM((PLANES, 2, SIDE, rows, cap), bf),
            pltpu.VMEM((PLANES, 2, SIDE, rows, 128), F32),
            pltpu.VMEM((topk, rows), jnp.int32),
            pltpu.VMEM((topk, rows), F32),
            pltpu.VMEM((PLANES, 2, n, rows), F32),
            pltpu.VMEM((model_width, width), bf),
            pltpu.VMEM((model_width, width), bf),
            pltpu.VMEM((2, width, half), bf),
            pltpu.VMEM((PLANES, 2, SIDE * cap, width), bf),
            pltpu.VMEM((PLANES, SIDE, cap, half), bf),
            pltpu.VMEM((PLANES, 3, cap, half), bf),
            pltpu.VMEM((PLANES, 2, rows, half), bf),
            pltpu.VMEM((PLANES, rows, half), bf),
            pltpu.VMEM((len(LANDING), 2, rows, half), bf),
            dma((6,)),
            dma((2, PLANES, 2, PARTS)), dma((PLANES, PARTS)), dma((PLANES, 2, PARTS)),
            dma((PLANES, 3, PARTS)), dma((PLANES, 3, PARTS)),
            dma((PLANES, SIDE)), dma((PLANES, SIDE)),
            dma((PLANES,)), dma((PLANES,)),
            dma, dma,
            dma((3, PLANES, 2)), dma((PLANES, 2)),
            dma((PLANES, 3, PARTS)), dma((PLANES, 3, PARTS)),
            dma((PLANES, PARTS)), dma((PLANES, PARTS)),
            dma((PLANES, 2, PARTS)), dma((len(LANDING), 2, PARTS)),
        ],
        compiler_params=pltpu.CompilerParams(
            collective_id=0, has_side_effects=True, vmem_limit_bytes=60 << 20
        ),
        cost_estimate=pl.CostEstimate(
            flops=6 * n * cap * model_width * width, bytes_accessed=12 << 20,
            transcendentals=n * cap * width,
        ),
        name="planes",
    )(tokens, expert_ids.T, routing_gates.T, w_gate, w_up, w_down)


def solution(mesh):
    small = mesh.shape["ep"] == PLANES * SIDE and mesh.shape["etp"] == 2
    return jax.shard_map(
        plane_shards if small else plain_shards,
        mesh=mesh,
        in_specs=(
            P("ep", None),
            P("ep", None),
            P("ep", None),
            P("ep", None, "etp"),
            P("ep", None, "etp"),
            P("ep", "etp", None),
        ),
        out_specs=P("ep", "etp"),
        check_vma=False,
    )
```
